32 devices in a mesh: pts: 8 (over y, x, core), val: 4 (over z).
Axes of the slice: x: 2, y: 2, z: 4, core: 2. Of those that a mesh axis runs over, the one named last changes fastest.
Arguments:
- vectors: float32 [1, 512, 2048], P(None, 'val', 'pts'), may hold values from -6 to 6
- eval_energy: float32 [512], P('val'), may hold values from -2 to -0.2
- cond_energy: float32 [2048], P('pts'), may hold values from 0.2 to 2
- val_orbitals: float32 [512, 8192], P('pts', 'val'), may hold values from -0.25 to 0.25
- cond_orbitals: float32 [2048, 8192], P('val', 'pts'), may hold values from -0.125 to 0.125
- screened: float32 [8192, 8192], P('val', 'pts'), may hold values from -1.5 to 1.5
Outputs:
- filtered: float32 [1, 512, 2048], P(None, 'val', 'pts')
The draws below stay inside these ranges and needn't reach their ends.
All inputs are finite; a program needn't handle non-finite values.
Results may differ from the reference program's by a relative error of at most 0.00013.
Values sent between devices are 32-bit elements; how exact they have to be, the bound alone decides.
A program may use at most 128 MiB of HBM per device.

```python
import jax
import jax.numpy as jnp
from jax import lax

NV = 512
NC = 2048
NP = 8192
BATCH = 1
ITERS = 2


def block_levels(own_key, dims, pieces, low, top_value):
    def one(axis_at, parts):
        heights = jax.random.uniform(jax.random.fold_in(jax.random.fold_in(own_key, 6), axis_at), (parts,), jnp.float32, low / len(pieces), top_value / len(pieces))
        return jnp.repeat(jnp.exp(heights), dims[axis_at] // parts).reshape((-1,) + (1,) * (len(dims) - axis_at - 1))

    level = one(*pieces[0])
    for cut in pieces[1:]:
        level = level * one(*cut)
    return level


def scatter_about(stream_key, dims, spread, bound, cuts=(), dtype=jnp.bfloat16):
    loudness = block_levels(stream_key, dims, cuts, -0.22, 0.18) if cuts else 1.0
    array = jax.random.normal(stream_key, dims, jnp.float32) * spread * loudness
    return jnp.minimum(jnp.maximum(array, -bound), bound).astype(dtype)


def setup_inputs(seed: int = 0) -> dict:
    key_list = jax.random.split(jax.random.key(seed), 7)
    vectors = scatter_about(key_list[0], (BATCH, NV, NC), 1.0, 6.0, ((1, 4), (2, 8)), jnp.float32)
    eval_energy = jnp.clip(-2.0 + 1.8 * jax.random.uniform(key_list[1], (NV,), jnp.float32) ** block_levels(key_list[1], (NV,), ((0, 4),), -0.2, 0.2), -2.0, -0.2)
    cond_energy = jnp.clip(0.2 + 1.8 * jax.random.uniform(key_list[2], (NC,), jnp.float32) ** block_levels(key_list[2], (NC,), ((0, 8),), -0.2, 0.2), 0.2, 2.0)
    val_orbitals = scatter_about(key_list[3], (NV, NP), NV ** -0.5, 0.25, ((0, 8), (1, 4)), jnp.float32)
    cond_orbitals = scatter_about(key_list[4], (NC, NP), NC ** -0.5, 0.125, ((0, 4), (1, 8)), jnp.float32)
    screened = scatter_about(key_list[5], (NP, NP), (NP * NP // (4 * NV * NC)) ** -0.5, 1.5, ((0, 4), (1, 8)), jnp.float32)
    return dict(vectors=vectors, eval_energy=eval_energy, cond_energy=cond_energy, val_orbitals=val_orbitals, cond_orbitals=cond_orbitals, screened=screened)


CENTER = 2.2
HALF_WIDTH = 2.0


def apply_direct(vec, val_orbitals, cond_orbitals, screened):
    highest = lax.Precision.HIGHEST

    def single(x):
        pair = jnp.dot(x, cond_orbitals, precision=highest, preferred_element_type=jnp.float32)
        mixed = jnp.dot(val_orbitals.T, pair, precision=highest, preferred_element_type=jnp.float32)
        weighted = mixed * screened
        back = jnp.dot(val_orbitals, weighted, precision=highest, preferred_element_type=jnp.float32)
        return jnp.dot(back, cond_orbitals.T, precision=highest, preferred_element_type=jnp.float32)

    return lax.map(single, vec)


def reference(vectors, eval_energy, cond_energy, val_orbitals, cond_orbitals, screened):
    ediff = cond_energy[None, None, :] - eval_energy[None, :, None]
    older = vectors
    newer = vectors
    for step in range(ITERS):
        hamil = ediff * newer - apply_direct(newer, val_orbitals, cond_orbitals, screened)
        scaled = (hamil - CENTER * newer) / HALF_WIDTH
        if step == 0:
            following = scaled
        else:
            following = 2.0 * scaled - older
        older = newer
        newer = following
    return newer
```

```python
import functools

import jax
import jax.numpy as jnp
from jax import lax
from jax.experimental import pallas as pl
from jax.experimental.pallas import tpu as pltpu
from jax.sharding import PartitionSpec as P

ITERS = 2
PIECES = 32
PIECES_AHEAD = 6

CENTER = 2.2
HALF_WIDTH = 2.0

LANES = 128
QC = 256
VMEM_BYTES = 67_043_328


def dot(dims, a, b):
    return lax.dot_general(
        a, b, (dims, ((), ())), precision=lax.Precision.HIGH, preferred_element_type=jnp.float32
    )


def line_kernel(axis, count, part_ref, out_ref, came, last, came_send, came_recv, last_send, last_recv):
    at = lax.axis_index(axis)
    half = count // 2
    left = at < half
    inner = jnp.where(left, at + 1, at - 1)
    outer = jnp.where(left, at - 1, at + 1)
    edge = (at == 0) | (at == count - 1)
    middle = (at == half - 1) | (at == half)
    pieces = part_ref.shape[0]

    def copy(source, target, send, recv, to):
        return pltpu.make_async_remote_copy(
            src_ref=source, dst_ref=target, send_sem=send, recv_sem=recv,
            device_id={axis: to}, device_id_type=pl.DeviceIdType.MESH,
        )

    def to_inner(t):
        return copy(out_ref.at[t], came.at[t], came_send.at[t], came_recv.at[t], inner)

    def across(t):
        return copy(out_ref.at[t], last.at[t], came_send.at[t], last_recv.at[t], inner)

    def to_outer(t):
        return copy(last.at[t], last.at[t], last_send.at[t], last_recv.at[t], outer)

    barrier = pltpu.get_barrier_semaphore()
    pl.semaphore_signal(barrier, inc=1, device_id={axis: inner}, device_id_type=pl.DeviceIdType.MESH)

    @pl.when(jnp.logical_not(edge))
    def _():
        pl.semaphore_signal(
            barrier, inc=1, device_id={axis: outer}, device_id_type=pl.DeviceIdType.MESH
        )
        pl.semaphore_wait(barrier, 2)

    @pl.when(edge)
    def _():
        pl.semaphore_wait(barrier, 1)

    def inward(t, carry):
        out_ref[t] = part_ref[t]

        @pl.when(jnp.logical_not(edge))
        def _():
            to_inner(t).wait_recv()
            out_ref[t] = part_ref[t] + came[t]

        @pl.when(middle)
        def _():
            across(t).start()

        @pl.when(jnp.logical_not(middle))
        def _():
            to_inner(t).start()

        return carry

    def outward(t, carry):
        across(t).wait_recv()

        @pl.when(middle)
        def _():
            last[t] = last[t] + out_ref[t]

        @pl.when(jnp.logical_not(edge))
        def _():
            to_outer(t).start()

        to_inner(t).wait_send()
        out_ref[t] = last[t]
        return carry

    def drain(t, carry):
        @pl.when(jnp.logical_not(edge))
        def _():
            to_outer(t).wait_send()

        return carry

    @pl.when(edge)
    def _():
        lax.fori_loop(0, pieces, inward, 0)
        lax.fori_loop(0, pieces, outward, 0)

    @pl.when(jnp.logical_not(edge))
    def _():
        def both(t, carry):
            inward(t, carry)
            return outward(t - PIECES_AHEAD, carry)

        lax.fori_loop(0, PIECES_AHEAD, inward, 0)
        lax.fori_loop(PIECES_AHEAD, pieces, both, 0)
        lax.fori_loop(pieces - PIECES_AHEAD, pieces, outward, 0)

    lax.fori_loop(0, pieces, drain, 0)


def line_sum(part, axis, count):
    if count == 1:
        return part
    if count % 2:
        return lax.psum(part, axis)
    rows, columns = part.shape
    cut = (PIECES, rows // PIECES, columns)
    total = pl.pallas_call(
        functools.partial(line_kernel, axis, count),
        out_shape=jax.ShapeDtypeStruct(cut, jnp.float32),
        in_specs=[pl.BlockSpec(memory_space=pltpu.VMEM)],
        out_specs=pl.BlockSpec(memory_space=pltpu.VMEM),
        scratch_shapes=[pltpu.VMEM(cut, jnp.float32)] * 2 + [pltpu.SemaphoreType.DMA((PIECES,))] * 4,
        compiler_params=pltpu.CompilerParams(collective_id=0, has_side_effects=True),
    )(part.reshape(cut))
    return total.reshape(part.shape)


def cube_sum(part, axis, count, order):
    at = lax.axis_index(axis)
    for bit in order:
        pairs = [(i, i ^ (1 << bit)) for i in range(count)]
        mine = (at >> bit) & 1
        rows = part.shape[0] // 2
        gone = lax.dynamic_slice_in_dim(part, (1 - mine) * rows, rows, 0)
        kept = lax.dynamic_slice_in_dim(part, mine * rows, rows, 0)
        part = kept + lax.ppermute(gone, axis, pairs)
    for bit in reversed(order):
        pairs = [(i, i ^ (1 << bit)) for i in range(count)]
        mine = (at >> bit) & 1
        got = lax.ppermute(part, axis, pairs)
        part = jnp.where(
            mine == 0, jnp.concatenate([part, got], 0), jnp.concatenate([got, part], 0)
        )
    return part


def plane_sum(part, axis, count):
    if count & (count - 1):
        return lax.psum(part, axis)
    bits = list(range(count.bit_length() - 1))
    other = bits[:1] + bits[1:][::-1]
    mid = part.shape[0] // 2
    return jnp.concatenate(
        [cube_sum(part[:mid], axis, count, bits), cube_sum(part[mid:], axis, count, other)], 0
    )


def per_device(
    n_pts, n_val, vectors, eval_energy, cond_energy, val_orbitals, cond_orbitals, screened
):
    bands, width = vectors.shape[1], vectors.shape[2]
    own = cond_orbitals.shape[0]
    per = own // width
    j, p = lax.axis_index("val"), lax.axis_index("pts")
    mine = (p // per) == j
    place = (p % per) * width

    val_whole = lax.all_gather(val_orbitals, "pts", axis=0, tiled=True)

    extra = jnp.stack([cond_energy, jnp.pad(eval_energy, (0, width - bands))])
    extra = jnp.pad(extra, ((0, 6), (0, 0)))
    held = lax.all_gather(jnp.concatenate([vectors[0], extra]), "val", axis=0)
    eval_whole = held[:, bands + 1, :bands].reshape(-1)
    rows = held[:, :bands].reshape(-1, width)
    valence = rows.shape[0]
    rows = jnp.concatenate([rows, jnp.pad(cond_energy[None], ((0, 16 * n_pts - 1), (0, 0)))])
    spread = lax.dynamic_update_slice(
        jnp.zeros((rows.shape[0], own), jnp.float32),
        jnp.where(mine, rows, 0.0),
        (jnp.zeros_like(place), place),
    )
    spread = plane_sum(spread, "pts", n_pts)
    older = newer = spread[:valence]
    ediff = spread[valence][None, :] - eval_whole[:, None]

    for step in range(ITERS):
        pair = line_sum(dot(((1,), (0,)), newer, cond_orbitals), "val", n_val)
        weighted = dot(((0,), (0,)), val_whole, pair) * screened
        back = line_sum(dot(((1,), (0,)), val_whole, weighted), "val", n_val)
        direct = dot(((1,), (1,)), back, cond_orbitals)
        direct = plane_sum(direct, "pts", n_pts)
        hamil = ediff * newer - direct
        scaled = (hamil - CENTER * newer) / HALF_WIDTH
        if step == 0:
            following = scaled
        else:
            following = 2.0 * scaled - older
        older = newer
        newer = following

    out = lax.dynamic_slice_in_dim(newer, place, width, 1)
    out = lax.psum_scatter(jnp.where(mine, out, 0.0), "val", scatter_dimension=0, tiled=True)
    return out[None]


def split(x):
    high = x.astype(jnp.bfloat16)
    return high, (x - high.astype(jnp.float32)).astype(jnp.bfloat16)


def product(dims, a, b):
    def one(left, right):
        return lax.dot_general(left, right, (dims, ((), ())), preferred_element_type=jnp.float32)

    return one(a[0], b[0]) + one(a[0], b[1]) + one(a[1], b[0])


def spans(bits):
    offsets = [0]
    for bit in bits:
        offsets = offsets + [offset | (1 << bit) for offset in offsets]
    return offsets


def fused_kernel(
    n_pts, n_val,
    x_ref, e_ref, cond_ref, v_ref, c_ref, w_ref, out_ref,
    cf, ch, cl, wf, vf, vh, vl, xf, xh, xl, ph, pl_, zh, zl, df, near, far, zin, zx, fin, fx, xo, ef,
    local, zs, zr, zsx, zrx, vls, vlr, vcs, vcr, als, alr, acs, acr, rls, rlr, rcs, rcr, hs, hr,
):
    p, j = lax.axis_index("pts"), lax.axis_index("val")
    MESH = pl.DeviceIdType.MESH
    last = n_val - 1
    half = n_val // 2
    depth = jnp.minimum(j, last - j)
    inner = jnp.where(j < half, j + 1, j - 1)
    outer = jnp.where(j < half, j - 1, j + 1)
    bits = list(range(1, n_pts.bit_length() - 1))
    m = len(bits)
    orders = [bits[a:] + bits[:a] for a in range(m)]
    nv, cw = df.shape[1], df.shape[2]
    vb = nv // n_val
    nk, cr, qc = cf.shape[1], cf.shape[2], cf.shape[3]
    nn, q = wf.shape
    nc = ch.shape[0]
    vr = vf.shape[1]
    groups = 2
    gr = nv // groups
    near_owners = [i << 1 for i in range(n_pts // 2)]

    def remote(source, target, send, recv, **to):
        return pltpu.make_async_remote_copy(
            src_ref=source, dst_ref=target, send_sem=send, recv_sem=recv,
            device_id=to, device_id_type=MESH,
        )

    def start(copies):
        for copy in copies:
            copy.start()

    def wait(copies):
        for copy in copies:
            copy.wait()

    def gather_link(buf, row0, size, step, ident, send, recv):
        out = []
        for a, order in enumerate(orders):
            rows = pl.ds(row0 + a * (size // m), size // m)
            for i, d in enumerate(spans(order[:step])):
                at = (1 << step) - 1 + i
                block = buf.at[p ^ d, rows]
                out.append(remote(block, block, send.at[ident, a, at], recv.at[ident, a, at],
                                  pts=p ^ (1 << order[step])))
        return out

    def gather_near(buf, row0, size, ident, send, recv):
        out = []
        for i, d in enumerate(near_owners):
            block = buf.at[p ^ d, pl.ds(row0, size)]
            out.append(remote(block, block, send.at[ident, i], recv.at[ident, i], pts=p ^ 1))
        return out

    def reduce_near(c):
        rows = pl.ds(c * vb, vb)
        return [
            remote(df.at[p ^ 1 ^ d, rows], near.at[i, rows], rcs.at[c, i], rcr.at[c, i], pts=p ^ 1)
            for i, d in enumerate(near_owners)
        ]

    def reduce_link(c, step):
        out = []
        for a, order in enumerate(orders):
            rows = pl.ds(c * vb + a * (vb // m), vb // m)
            to = p ^ (1 << order[step])
            for i, d in enumerate(spans(order[:step])):
                at = (1 << step) - 1 + i
                out.append(remote(df.at[to ^ d, rows], far.at[at, rows], rls.at[c, a, at],
                                  rlr.at[c, a, at], pts=to))
        return out

    def add_near(c):
        rows = pl.ds(c * vb, vb)
        for i, d in enumerate(near_owners):
            df[p ^ d, rows] = df[p ^ d, rows] + near[i, rows]

    def add_link(c, step):
        for a, order in enumerate(orders):
            rows = pl.ds(c * vb + a * (vb // m), vb // m)
            for i, d in enumerate(spans(order[:step])):
                at = (1 << step) - 1 + i
                df[p ^ d, rows] = df[p ^ d, rows] + far[at, rows]

    def line_block(sign, r, sending):
        if sign > 0:
            block = j - r if sending else j - 1 - r
            edge = (j < last) if sending else (j > 0)
            ok = edge & (block >= 0)
        else:
            block = j + r if sending else j + 1 + r
            edge = (j > 0) if sending else (j < last)
            ok = edge & (block <= last)
        return jnp.clip(block, 0, last), ok

    def line_copy(item, sign, r, sending, first=None):
        block, ok = line_block(sign, r, sending)
        target, send, recv = item(block, 0 if sign > 0 else 1, r)
        source = first if (first is not None and r == 0 and sending) else target
        to = jnp.clip(j + sign, 0, last)
        return remote(source, target, send, recv, val=to), ok

    def x_item(block, way, r):
        return xf.at[p, pl.ds(block * vb, vb)], zsx.at[0, way, r], zrx.at[0, way, r]

    def e_item(block, way, r):
        return ef.at[block], zsx.at[1, way, r], zrx.at[1, way, r]

    def c_item(k):
        def item(block, way, r):
            return cf.at[block, k], zs.at[way, r, k], zr.at[way, r, k]

        return item

    def line_do(what, item, sign, r, first=None):
        copy, ok = line_copy(item, sign, r, what != "recv", first)

        @pl.when(ok)
        def _():
            if what == "start":
                copy.start()
            elif what == "recv":
                copy.wait_recv()
            else:
                copy.wait_send()

    def columns(k):
        return pl.ds(pl.multiple_of(k * qc, qc), qc)

    own = [
        pltpu.make_async_copy(v_ref, vf.at[p], local.at[0]),
        pltpu.make_async_copy(x_ref, xf.at[p, pl.ds(j * vb, vb)], local.at[1]),
        pltpu.make_async_copy(e_ref, ef.at[j], local.at[2]),
        pltpu.make_async_copy(x_ref, xo, local.at[3]),
        pltpu.make_async_copy(w_ref, wf, local.at[4]),
    ]
    mine = [
        pltpu.make_async_copy(c_ref.at[:, pl.ds(k * qc, qc)], cf.at[j, k], local.at[5 + k])
        for k in range(nk)
    ]
    start(own[:4])
    start(mine)
    start(own[4:])

    barrier = pltpu.get_barrier_semaphore()
    for bit in [0] + bits:
        pl.semaphore_signal(barrier, inc=1, device_id={"pts": p ^ (1 << bit)}, device_id_type=MESH)

    @pl.when(j > 0)
    def _():
        pl.semaphore_signal(barrier, inc=1, device_id={"val": j - 1}, device_id_type=MESH)

    @pl.when(j < last)
    def _():
        pl.semaphore_signal(barrier, inc=1, device_id={"val": j + 1}, device_id_type=MESH)

    @pl.when(depth == 0)
    def _():
        pl.semaphore_wait(barrier, m + 2)

    @pl.when(depth > 0)
    def _():
        pl.semaphore_wait(barrier, m + 3)

    for sign in (1, -1):
        line_do("start", x_item, sign, 0, x_ref)
        line_do("start", e_item, sign, 0, e_ref)
    own[0].wait()
    start(gather_link(vf, 0, vr, 0, 0, vls, vlr))
    for k in range(nk):
        for sign in (1, -1):
            line_do("start", c_item(k), sign, 0, c_ref.at[:, pl.ds(k * qc, qc)])
    for r in range(n_val - 1):
        for sign in (1, -1):
            for item in (x_item, e_item):
                line_do("recv", item, sign, r)
                if r + 1 < n_val - 1:
                    line_do("start", item, sign, r + 1)
    own[1].wait()
    start(gather_link(xf, 0, nv, 0, 0, als, alr))
    for step in range(1, m):
        wait(gather_link(vf, 0, vr, step - 1, 0, vls, vlr))
        start(gather_link(vf, 0, vr, step, 0, vls, vlr))
        wait(gather_link(xf, 0, nv, step - 1, 0, als, alr))
        start(gather_link(xf, 0, nv, step, 0, als, alr))
    wait(gather_link(vf, 0, vr, m - 1, 0, vls, vlr))
    start(gather_near(vf, 0, vr, 0, vcs, vcr))

    def split_c(block, k):
        rows = pl.ds(pl.multiple_of(block * cr, cr), cr)
        high, low = split(cf[block, k])
        ch[rows, columns(k)] = high
        cl[rows, columns(k)] = low

    for k in range(nk):
        mine[k].wait()

    def split_own(k, carry):
        split_c(j, k)
        return carry

    lax.fori_loop(0, nk, split_own, 0)
    wait(gather_near(vf, 0, vr, 0, vcs, vcr))

    def split_v(o, carry):
        rows = pl.ds(pl.multiple_of(o * vr, vr), vr)
        high, low = split(vf[o])
        vh[rows] = high
        vl[rows] = low
        return carry

    lax.fori_loop(0, n_pts, split_v, 0)
    wait(gather_link(xf, 0, nv, m - 1, 0, als, alr))
    start(gather_near(xf, 0, nv, 0, acs, acr))
    wait(gather_near(xf, 0, nv, 0, acs, acr))

    def split_x(row0, size):
        rows = pl.ds(row0, size)
        for b in range(n_pts):
            high, low = split(xf[b, rows])
            xh[rows, b * cw:(b + 1) * cw] = high
            xl[rows, b * cw:(b + 1) * cw] = low

    def split_rows(t, carry):
        split_x(pl.multiple_of(t * vb, vb), vb)
        return carry

    lax.fori_loop(0, n_val, split_rows, 0)
    for r in range(n_val - 1):
        for sign in (1, -1):
            for item in (x_item, e_item):
                line_do("send", item, sign, r, x_ref if item is x_item else e_ref)
    for copy in own[2:]:
        copy.wait()

    def arrive(r, k):
        for sign in (1, -1):
            line_do("recv", c_item(k), sign, r)
            if r + 1 < n_val - 1:
                line_do("start", c_item(k), sign, r + 1)
        for sign in (1, -1):
            block, ok = line_block(sign, r, False)

            @pl.when(ok)
            def _():
                split_c(block, k)

    def pass_on(r):
        def body(k, carry):
            arrive(r, k)
            return carry

        lax.fori_loop(0, nk, body, 0)

    for r in range(n_val - 2):
        pass_on(r)

    nt = min(512, nn)

    def store(high, low, at, value):
        a, b = split(value)
        high[at] = a
        low[at] = b

    def column(k, carry):
        arrive(n_val - 2, k)
        cols = columns(k)

        def pair(t, c):
            rows = pl.ds(pl.multiple_of(t * gr, gr), gr)
            store(ph, pl_, (rows, cols), product(
                ((1,), (0,)), (xh[rows], xl[rows]), (ch[:, cols], cl[:, cols])))
            return c

        lax.fori_loop(0, groups, pair, 0)

        def mixed(t, c):
            at = pl.ds(pl.multiple_of(t * nt, nt), nt)
            value = product(((0,), (0,)), (vh[:, at], vl[:, at]), (ph[:, cols], pl_[:, cols]))
            store(zh, zl, (at, cols), value * wf[at, cols])
            return c

        lax.fori_loop(0, nn // nt, mixed, 0)

        def back(t, c):
            rows = pl.ds(pl.multiple_of(t * gr, gr), gr)
            store(ph, pl_, (rows, cols), product(
                ((1,), (0,)), (vh[rows], vl[rows]), (zh[:, cols], zl[:, cols])))
            return c

        lax.fori_loop(0, groups, back, 0)
        return carry

    lax.fori_loop(0, nk, column, 0)

    def sent(k, carry):
        for r in range(n_val - 1):
            for sign in (1, -1):
                line_do("send", c_item(k), sign, r, c_ref.at[:, pl.ds(0, qc)])
        return carry

    lax.fori_loop(0, nk, sent, 0)

    def direct(g, flip):
        rows = pl.ds(g * gr, gr)

        def body(i, c):
            owner = p ^ flip ^ (2 * i)
            at = pl.ds(pl.multiple_of(owner * cw, cw), cw)
            df[owner, rows] = product(
                ((1,), (1,)), (ph[rows], pl_[rows]), (ch[at], cl[at]))
            return c

        lax.fori_loop(0, n_pts // 2, body, 0)

    def reduce_stages(c):
        stages = [lambda: (wait(reduce_near(c)), add_near(c), start(reduce_link(c, m - 1)))]
        for step in range(m - 1, 0, -1):
            stages.append(lambda step=step: (
                wait(reduce_link(c, step)), add_link(c, step), start(reduce_link(c, step - 1))))
        return stages

    def last_add(c):
        wait(reduce_link(c, 0))
        add_link(c, 0)

    def own_sum(c):
        rows = pl.ds(c * vb, vb)
        return df[p, rows]

    def scaled(c, newer, total):
        ediff = cond_ref[...] - ef[c][:, 0:1]
        hamil = ediff * newer - total
        return (hamil - CENTER * newer) / HALF_WIDTH

    def spread_stages(c):
        rows = pl.ds(c * vb, vb)
        stages = reduce_stages(c)
        source = df.at[p, rows]

        def to_inner():
            return remote(source, zin.at[rows], hs.at[c, 0], hr.at[c, 0], val=inner)

        def across():
            return remote(source, zx.at[rows], hs.at[c, 0], hr.at[c, 1], val=inner)

        def to_outer():
            return remote(zx.at[rows], zx.at[rows], hs.at[c, 1], hr.at[c, 1], val=outer)

        def inward(i):
            if i == 0:
                last_add(c)

            @pl.when(depth == i)
            def _():
                if i > 0:
                    to_inner().wait_recv()
                    df[p, rows] = df[p, rows] + zin[rows]
                (across() if i == half - 1 else to_inner()).start()

        def outward(i):
            @pl.when(depth == i)
            def _():
                across().wait_recv()
                if i == half - 1:
                    zx[rows] = zx[rows] + df[p, rows]
                if i > 0:
                    to_outer().start()

        def following():
            across().wait_send()

            @pl.when(depth > 0)
            def _():
                to_outer().wait_send()

            newer = xf[p, rows]
            xf[p, rows] = scaled(c, newer, zx[rows])
            start(gather_link(xf, c * vb, vb, 0, c, als, alr))

        for i in range(half):
            stages.append(lambda i=i: inward(i))
        for i in range(half - 1, 0, -1):
            stages.append(lambda i=i: outward(i))
        stages.append(lambda: (outward(0), following()))
        for step in range(1, m):
            stages.append(lambda step=step: (
                wait(gather_link(xf, c * vb, vb, step - 1, c, als, alr)),
                start(gather_link(xf, c * vb, vb, step, c, als, alr))))
        stages.append(lambda: (
            wait(gather_link(xf, c * vb, vb, m - 1, c, als, alr)),
            start(gather_near(xf, c * vb, vb, c, acs, acr))))
        stages.append(lambda: (
            wait(gather_near(xf, c * vb, vb, c, acs, acr)), split_x(c * vb, vb)))
        return stages

    def final_stages(c):
        rows = pl.ds(c * vb, vb)
        stages = reduce_stages(c)

        def right():
            return remote(df.at[p, rows], fin.at[rows], hs.at[c, 0], hr.at[c, 0],
                          val=jnp.minimum(j + 1, last))

        def left():
            return remote(df.at[p, rows], fx.at[rows], hs.at[c, 0], hr.at[c, 1],
                          val=jnp.maximum(j - 1, 0))

        def step(i):
            if i == 0:
                last_add(c)
            if i < c:
                @pl.when(j == i)
                def _():
                    if i > 0:
                        right().wait_recv()
                        df[p, rows] = df[p, rows] + fin[rows]
                    right().start()
            if last - i > c:
                @pl.when(j == last - i)
                def _():
                    if i > 0:
                        left().wait_recv()
                        df[p, rows] = df[p, rows] + fx[rows]
                    left().start()

        def finish():
            @pl.when(j == c)
            def _():
                total = df[p, rows]
                if c > 0:
                    right().wait_recv()
                    total = total + fin[rows]
                if c < last:
                    left().wait_recv()
                    total = total + fx[rows]
                out_ref[...] = 2.0 * scaled(c, xf[p, rows], total) - xo[...]

            @pl.when(j != c)
            def _():
                right().wait_send()

        for i in range(max(c, last - c)):
            stages.append(lambda i=i: step(i))
        stages.append(finish)
        return stages

    per = n_val // groups

    def reduction(stages_of, order, fillers, begin):
        direct(0, 1)
        for c in order[:per]:
            start(reduce_near(c))
        direct(0, 0)
        todo = {c: (begin[at], stages_of(c)) for at, c in enumerate(order)}
        end = max(b + len(s) for b, s in todo.values())
        for tick in range(end):
            if fillers:
                fillers.pop(0)()
            for c in order:
                b, stages = todo[c]
                if 0 <= tick - b < len(stages):
                    stages[tick - b]()

    def near_rest(order):
        for c in order[per:]:
            start(reduce_near(c))

    order = list(range(n_val))
    begin = [t if t < per else t + 2 for t in range(n_val)]
    reduction(
        spread_stages, order,
        [lambda: direct(1, 1), lambda: near_rest(order), lambda: direct(1, 0)], begin)

    qt = min(512, q)

    def pair(t, c):
        g, at = t // (q // qt), pl.ds(pl.multiple_of((t % (q // qt)) * qt, qt), qt)
        rows = pl.ds(pl.multiple_of(g * gr, gr), gr)
        store(ph, pl_, (rows, at), product(
            ((1,), (0,)), (xh[rows], xl[rows]), (ch[:, at], cl[:, at])))
        return c

    lax.fori_loop(0, groups * (q // qt), pair, 0)

    def mixed(t, c):
        at = pl.ds(pl.multiple_of((t // (q // qt)) * nt, nt), nt)
        cols = pl.ds(pl.multiple_of((t % (q // qt)) * qt, qt), qt)
        value = product(((0,), (0,)), (vh[:, at], vl[:, at]), (ph[:, cols], pl_[:, cols]))
        store(zh, zl, (at, cols), value * wf[at, cols])
        return c

    lax.fori_loop(0, (nn // nt) * (q // qt), mixed, 0)

    def back(g):
        def body(t, c):
            rows = pl.ds(g * gr, gr)
            at = pl.ds(pl.multiple_of(t * qt, qt), qt)
            store(ph, pl_, (rows, at), product(
                ((1,), (0,)), (vh[rows], vl[rows]), (zh[:, at], zl[:, at])))
            return c

        lax.fori_loop(0, q // qt, body, 0)

    back(0)
    order = order[:per] + order[per:][::-1]
    reduction(
        final_stages, order,
        [lambda: back(1), lambda: direct(1, 1), lambda: near_rest(order), lambda: direct(1, 0)],
        [t if t < per else t + 2 for t in range(n_val)])


def fused(n_pts, n_val, vectors, eval_energy, cond_energy, val_orbitals, cond_orbitals, screened):
    vb, cw = vectors.shape[1:]
    vr, nn = val_orbitals.shape
    cr, q = cond_orbitals.shape
    nv, nc = vb * n_val, cw * n_pts
    nk = q // QC
    m = n_pts.bit_length() - 2
    f32, bf16 = jnp.float32, jnp.bfloat16
    links = (1 << m) - 1
    any_, dma = pl.BlockSpec(memory_space=pl.ANY), pltpu.SemaphoreType.DMA
    vmem = pl.BlockSpec(memory_space=pltpu.VMEM)
    buffers = [
        ((n_val, nk, cr, QC), f32), ((nc, q), bf16), ((nc, q), bf16), ((nn, q), f32),
        ((n_pts, vr, nn), f32), ((nv, nn), bf16), ((nv, nn), bf16),
        ((n_pts, nv, cw), f32), ((nv, nc), bf16), ((nv, nc), bf16),
        ((nv, q), bf16), ((nv, q), bf16), ((nn, q), bf16), ((nn, q), bf16),
        ((n_pts, nv, cw), f32), ((n_pts // 2, nv, cw), f32), ((links, nv, cw), f32),
        ((nv, cw), f32), ((nv, cw), f32), ((nv, cw), f32), ((nv, cw), f32), ((vb, cw), f32),
        ((n_val, vb, LANES), f32),
    ]
    semaphores = [
        (5 + nk,), (2, n_val - 1, nk), (2, n_val - 1, nk), (2, 2, n_val - 1), (2, 2, n_val - 1),
        (1, m, links), (1, m, links), (1, n_pts // 2), (1, n_pts // 2),
        (n_val, m, links), (n_val, m, links), (n_val, n_pts // 2), (n_val, n_pts // 2),
        (n_val, m, links), (n_val, m, links), (n_val, n_pts // 2), (n_val, n_pts // 2),
        (n_val, 2), (n_val, 2),
    ]
    out = pl.pallas_call(
        functools.partial(fused_kernel, n_pts, n_val),
        out_shape=jax.ShapeDtypeStruct((vb, cw), f32),
        in_specs=[any_, any_, vmem, any_, any_, any_],
        out_specs=vmem,
        scratch_shapes=[pltpu.VMEM(*b) for b in buffers] + [dma(s) for s in semaphores],
        compiler_params=pltpu.CompilerParams(
            collective_id=0, has_side_effects=True, vmem_limit_bytes=VMEM_BYTES
        ),
    )(
        vectors[0], jnp.broadcast_to(eval_energy[:, None], (vb, LANES)), cond_energy[None],
        val_orbitals, cond_orbitals, screened,
    )
    return out[None]


def fits(n_pts, n_val, vectors, val_orbitals, cond_orbitals):
    vb, cw = vectors.shape[1:]
    vr, nn = val_orbitals.shape
    cr, q = cond_orbitals.shape
    nv, nc = vb * n_val, cw * n_pts
    m = n_pts.bit_length() - 2
    if n_pts & (n_pts - 1) or m < 1 or n_val % 2 or n_val < 2:
        return False
    if cw % LANES or q % QC or nn % 512 or vb % (16 * m) or vr % (16 * m) or cr % 16:
        return False
    held = 8 * nc * q + 8 * nn * q + 8 * nv * nn + 8 * nv * nc + 4 * nv * q
    held += 4 * nv * nc * 3 // 2 + 4 * nv * cw * ((1 << m) + 3)
    return held <= VMEM_BYTES - 3 * 2**20


def solution(mesh):
    placed = (
        P(None, "val", "pts"),
        P("val"),
        P("pts"),
        P("pts", "val"),
        P("val", "pts"),
        P("val", "pts"),
    )
    n_pts, n_val = mesh.shape["pts"], mesh.shape["val"]

    def body(vectors, eval_energy, cond_energy, val_orbitals, cond_orbitals, screened):
        run = fused if fits(n_pts, n_val, vectors, val_orbitals, cond_orbitals) else per_device
        return run(
            n_pts, n_val, vectors, eval_energy, cond_energy, val_orbitals, cond_orbitals, screened
        )

    return jax.shard_map(
        body, mesh=mesh, in_specs=placed, out_specs=P(None, "val", "pts"), check_vma=False
    )
```

```python
import functools

import jax
import jax.numpy as jnp
from jax import lax
from jax.experimental import pallas as pl
from jax.experimental.pallas import tpu as pltpu
from jax.sharding import PartitionSpec as P

ITERS = 2
PIECES = 32
PIECES_AHEAD = 6

CENTER = 2.2
HALF_WIDTH = 2.0

LANES = 128
QC = 256
SUB = 2
GAP = 2
VMEM_BYTES = 67_043_328


def dot(dims, a, b):
    return lax.dot_general(
        a, b, (dims, ((), ())), precision=lax.Precision.HIGH, preferred_element_type=jnp.float32
    )


def line_kernel(axis, count, part_ref, out_ref, came, last, came_send, came_recv, last_send, last_recv):
    at = lax.axis_index(axis)
    half = count // 2
    left = at < half
    inner = jnp.where(left, at + 1, at - 1)
    outer = jnp.where(left, at - 1, at + 1)
    edge = (at == 0) | (at == count - 1)
    middle = (at == half - 1) | (at == half)
    pieces = part_ref.shape[0]

    def copy(source, target, send, recv, to):
        return pltpu.make_async_remote_copy(
            src_ref=source, dst_ref=target, send_sem=send, recv_sem=recv,
            device_id={axis: to}, device_id_type=pl.DeviceIdType.MESH,
        )

    def to_inner(t):
        return copy(out_ref.at[t], came.at[t], came_send.at[t], came_recv.at[t], inner)

    def across(t):
        return copy(out_ref.at[t], last.at[t], came_send.at[t], last_recv.at[t], inner)

    def to_outer(t):
        return copy(last.at[t], last.at[t], last_send.at[t], last_recv.at[t], outer)

    barrier = pltpu.get_barrier_semaphore()
    pl.semaphore_signal(barrier, inc=1, device_id={axis: inner}, device_id_type=pl.DeviceIdType.MESH)

    @pl.when(jnp.logical_not(edge))
    def _():
        pl.semaphore_signal(
            barrier, inc=1, device_id={axis: outer}, device_id_type=pl.DeviceIdType.MESH
        )
        pl.semaphore_wait(barrier, 2)

    @pl.when(edge)
    def _():
        pl.semaphore_wait(barrier, 1)

    def inward(t, carry):
        out_ref[t] = part_ref[t]

        @pl.when(jnp.logical_not(edge))
        def _():
            to_inner(t).wait_recv()
            out_ref[t] = part_ref[t] + came[t]

        @pl.when(middle)
        def _():
            across(t).start()

        @pl.when(jnp.logical_not(middle))
        def _():
            to_inner(t).start()

        return carry

    def outward(t, carry):
        across(t).wait_recv()

        @pl.when(middle)
        def _():
            last[t] = last[t] + out_ref[t]

        @pl.when(jnp.logical_not(edge))
        def _():
            to_outer(t).start()

        to_inner(t).wait_send()
        out_ref[t] = last[t]
        return carry

    def drain(t, carry):
        @pl.when(jnp.logical_not(edge))
        def _():
            to_outer(t).wait_send()

        return carry

    @pl.when(edge)
    def _():
        lax.fori_loop(0, pieces, inward, 0)
        lax.fori_loop(0, pieces, outward, 0)

    @pl.when(jnp.logical_not(edge))
    def _():
        def both(t, carry):
            inward(t, carry)
            return outward(t - PIECES_AHEAD, carry)

        lax.fori_loop(0, PIECES_AHEAD, inward, 0)
        lax.fori_loop(PIECES_AHEAD, pieces, both, 0)
        lax.fori_loop(pieces - PIECES_AHEAD, pieces, outward, 0)

    lax.fori_loop(0, pieces, drain, 0)


def line_sum(part, axis, count):
    if count == 1:
        return part
    if count % 2:
        return lax.psum(part, axis)
    rows, columns = part.shape
    cut = (PIECES, rows // PIECES, columns)
    total = pl.pallas_call(
        functools.partial(line_kernel, axis, count),
        out_shape=jax.ShapeDtypeStruct(cut, jnp.float32),
        in_specs=[pl.BlockSpec(memory_space=pltpu.VMEM)],
        out_specs=pl.BlockSpec(memory_space=pltpu.VMEM),
        scratch_shapes=[pltpu.VMEM(cut, jnp.float32)] * 2 + [pltpu.SemaphoreType.DMA((PIECES,))] * 4,
        compiler_params=pltpu.CompilerParams(collective_id=0, has_side_effects=True),
    )(part.reshape(cut))
    return total.reshape(part.shape)


def cube_sum(part, axis, count, order):
    at = lax.axis_index(axis)
    for bit in order:
        pairs = [(i, i ^ (1 << bit)) for i in range(count)]
        mine = (at >> bit) & 1
        rows = part.shape[0] // 2
        gone = lax.dynamic_slice_in_dim(part, (1 - mine) * rows, rows, 0)
        kept = lax.dynamic_slice_in_dim(part, mine * rows, rows, 0)
        part = kept + lax.ppermute(gone, axis, pairs)
    for bit in reversed(order):
        pairs = [(i, i ^ (1 << bit)) for i in range(count)]
        mine = (at >> bit) & 1
        got = lax.ppermute(part, axis, pairs)
        part = jnp.where(
            mine == 0, jnp.concatenate([part, got], 0), jnp.concatenate([got, part], 0)
        )
    return part


def plane_sum(part, axis, count):
    if count & (count - 1):
        return lax.psum(part, axis)
    bits = list(range(count.bit_length() - 1))
    other = bits[:1] + bits[1:][::-1]
    mid = part.shape[0] // 2
    return jnp.concatenate(
        [cube_sum(part[:mid], axis, count, bits), cube_sum(part[mid:], axis, count, other)], 0
    )


def per_device(
    n_pts, n_val, vectors, eval_energy, cond_energy, val_orbitals, cond_orbitals, screened
):
    bands, width = vectors.shape[1], vectors.shape[2]
    own = cond_orbitals.shape[0]
    per = own // width
    j, p = lax.axis_index("val"), lax.axis_index("pts")
    mine = (p // per) == j
    place = (p % per) * width

    val_whole = lax.all_gather(val_orbitals, "pts", axis=0, tiled=True)

    extra = jnp.stack([cond_energy, jnp.pad(eval_energy, (0, width - bands))])
    extra = jnp.pad(extra, ((0, 6), (0, 0)))
    held = lax.all_gather(jnp.concatenate([vectors[0], extra]), "val", axis=0)
    eval_whole = held[:, bands + 1, :bands].reshape(-1)
    rows = held[:, :bands].reshape(-1, width)
    valence = rows.shape[0]
    rows = jnp.concatenate([rows, jnp.pad(cond_energy[None], ((0, 16 * n_pts - 1), (0, 0)))])
    spread = lax.dynamic_update_slice(
        jnp.zeros((rows.shape[0], own), jnp.float32),
        jnp.where(mine, rows, 0.0),
        (jnp.zeros_like(place), place),
    )
    spread = plane_sum(spread, "pts", n_pts)
    older = newer = spread[:valence]
    ediff = spread[valence][None, :] - eval_whole[:, None]

    for step in range(ITERS):
        pair = line_sum(dot(((1,), (0,)), newer, cond_orbitals), "val", n_val)
        weighted = dot(((0,), (0,)), val_whole, pair) * screened
        back = line_sum(dot(((1,), (0,)), val_whole, weighted), "val", n_val)
        direct = dot(((1,), (1,)), back, cond_orbitals)
        direct = plane_sum(direct, "pts", n_pts)
        hamil = ediff * newer - direct
        scaled = (hamil - CENTER * newer) / HALF_WIDTH
        if step == 0:
            following = scaled
        else:
            following = 2.0 * scaled - older
        older = newer
        newer = following

    out = lax.dynamic_slice_in_dim(newer, place, width, 1)
    out = lax.psum_scatter(jnp.where(mine, out, 0.0), "val", scatter_dimension=0, tiled=True)
    return out[None]


def split(x):
    high = x.astype(jnp.bfloat16)
    return high, (x - high.astype(jnp.float32)).astype(jnp.bfloat16)


def product(dims, a, b):
    def one(left, right):
        return lax.dot_general(left, right, (dims, ((), ())), preferred_element_type=jnp.float32)

    return one(a[0], b[0]) + one(a[0], b[1]) + one(a[1], b[0])


def spans(bits):
    offsets = [0]
    for bit in bits:
        offsets = offsets + [offset | (1 << bit) for offset in offsets]
    return offsets


def fused_kernel(
    n_pts, n_val,
    x_ref, e_ref, cond_ref, v_ref, c_ref, w_ref, out_ref,
    cf, ch, cl, wf, vf, vh, vl, xf, xh, xl, ph, pl_, zh, zl, near, far, zin, zx, fin, fx, xo, ef,
    local, zs, zr, zsx, zrx, vls, vlr, vcs, vcr, als, alr, acs, acr, rls, rlr, rcs, rcr, hs, hr,
):
    p, j = lax.axis_index("pts"), lax.axis_index("val")
    MESH = pl.DeviceIdType.MESH
    last = n_val - 1
    half = n_val // 2
    depth = jnp.minimum(j, last - j)
    inner = jnp.where(j < half, j + 1, j - 1)
    outer = jnp.where(j < half, j - 1, j + 1)
    bits = list(range(1, n_pts.bit_length() - 1))
    m = len(bits)
    orders = [bits[a:] + bits[:a] for a in range(m)]
    df = vf
    nv, cw = df.shape[1], df.shape[2]
    vb = nv // n_val
    ck = vb // SUB
    chunks = n_val * SUB
    nk, cr, qc = cf.shape[1], cf.shape[2], cf.shape[3]
    nn, q = wf.shape
    nc = ch.shape[0]
    vr = nv // n_pts
    groups = 2
    gr = nv // groups
    near_owners = [i << 1 for i in range(n_pts // 2)]

    def remote(source, target, send, recv, **to):
        return pltpu.make_async_remote_copy(
            src_ref=source, dst_ref=target, send_sem=send, recv_sem=recv,
            device_id=to, device_id_type=MESH,
        )

    def start(copies):
        for copy in copies:
            copy.start()

    def wait(copies):
        for copy in copies:
            copy.wait()

    def x_block(owner, row0, size):
        return xf.at[owner, pl.ds(row0, size)]

    def v_block(owner, row0, size):
        return vf.at[:, pl.ds(pl.multiple_of(owner * vr + row0, size), size)]

    def gather_link(block_of, row0, size, step, ident, send, recv):
        out = []
        for a, order in enumerate(orders):
            for i, d in enumerate(spans(order[:step])):
                at = (1 << step) - 1 + i
                block = block_of(p ^ d, row0 + a * (size // m), size // m)
                out.append(remote(block, block, send.at[ident, a, at], recv.at[ident, a, at],
                                  pts=p ^ (1 << order[step])))
        return out

    def gather_near(block_of, row0, size, ident, send, recv):
        out = []
        for i, d in enumerate(near_owners):
            block = block_of(p ^ d, row0, size)
            out.append(remote(block, block, send.at[ident, i], recv.at[ident, i], pts=p ^ 1))
        return out

    def reduce_near(c):
        rows = pl.ds(c * ck, ck)
        return [
            remote(df.at[p ^ 1 ^ d, rows], near.at[i, rows], rcs.at[c, i], rcr.at[c, i], pts=p ^ 1)
            for i, d in enumerate(near_owners)
        ]

    def reduce_link(c, step):
        out = []
        for a, order in enumerate(orders):
            rows = pl.ds(c * ck + a * (ck // m), ck // m)
            to = p ^ (1 << order[step])
            for i, d in enumerate(spans(order[:step])):
                at = (1 << step) - 1 + i
                out.append(remote(df.at[to ^ d, rows], far.at[at, rows], rls.at[c, a, at],
                                  rlr.at[c, a, at], pts=to))
        return out

    def add_near(c):
        rows = pl.ds(c * ck, ck)
        for i, d in enumerate(near_owners):
            df[p ^ d, rows] = df[p ^ d, rows] + near[i, rows]

    def add_link(c, step):
        for a, order in enumerate(orders):
            rows = pl.ds(c * ck + a * (ck // m), ck // m)
            for i, d in enumerate(spans(order[:step])):
                at = (1 << step) - 1 + i
                df[p ^ d, rows] = df[p ^ d, rows] + far[at, rows]

    def line_block(sign, r, sending):
        if sign > 0:
            block = j - r if sending else j - 1 - r
            edge = (j < last) if sending else (j > 0)
            ok = edge & (block >= 0)
        else:
            block = j + r if sending else j + 1 + r
            edge = (j > 0) if sending else (j < last)
            ok = edge & (block <= last)
        return jnp.clip(block, 0, last), ok

    def line_copy(item, sign, r, sending, first=None):
        block, ok = line_block(sign, r, sending)
        target, send, recv = item(block, 0 if sign > 0 else 1, r)
        source = first if (first is not None and r == 0 and sending) else target
        to = jnp.clip(j + sign, 0, last)
        return remote(source, target, send, recv, val=to), ok

    def x_item(block, way, r):
        return xf.at[p, pl.ds(block * vb, vb)], zsx.at[0, way, r], zrx.at[0, way, r]

    def e_item(block, way, r):
        return ef.at[block], zsx.at[1, way, r], zrx.at[1, way, r]

    def c_item(k):
        def item(block, way, r):
            return cf.at[block, k], zs.at[way, r, k], zr.at[way, r, k]

        return item

    def line_do(what, item, sign, r, first=None):
        copy, ok = line_copy(item, sign, r, what != "recv", first)

        @pl.when(ok)
        def _():
            if what == "start":
                copy.start()
            elif what == "recv":
                copy.wait_recv()
            else:
                copy.wait_send()

    def columns(k):
        return pl.ds(pl.multiple_of(k * qc, qc), qc)

    own = [
        pltpu.make_async_copy(v_ref.at[:, pl.ds(t * cw, cw)], vf.at[t, pl.ds(p * vr, vr)],
                              local.at[4 + nk + t])
        for t in range(n_pts)
    ]
    first = [
        pltpu.make_async_copy(x_ref, xf.at[p, pl.ds(j * vb, vb)], local.at[0]),
        pltpu.make_async_copy(e_ref, ef.at[j], local.at[1]),
        pltpu.make_async_copy(x_ref, xo, local.at[2]),
        pltpu.make_async_copy(w_ref, wf, local.at[3]),
    ]
    mine = [
        pltpu.make_async_copy(c_ref.at[:, pl.ds(k * qc, qc)], cf.at[j, k], local.at[4 + k])
        for k in range(nk)
    ]
    start(own)
    start(first[:3])
    start(mine)
    start(first[3:])

    barrier = pltpu.get_barrier_semaphore()
    for bit in [0] + bits:
        pl.semaphore_signal(barrier, inc=1, device_id={"pts": p ^ (1 << bit)}, device_id_type=MESH)

    @pl.when(j > 0)
    def _():
        pl.semaphore_signal(barrier, inc=1, device_id={"val": j - 1}, device_id_type=MESH)

    @pl.when(j < last)
    def _():
        pl.semaphore_signal(barrier, inc=1, device_id={"val": j + 1}, device_id_type=MESH)

    @pl.when(depth == 0)
    def _():
        pl.semaphore_wait(barrier, m + 2)

    @pl.when(depth > 0)
    def _():
        pl.semaphore_wait(barrier, m + 3)

    def send_c(k):
        for sign in (1, -1):
            line_do("start", c_item(k), sign, 0, c_ref.at[:, pl.ds(k * qc, qc)])

    def x_round(r):
        for sign in (1, -1):
            for item in (x_item, e_item):
                line_do("recv", item, sign, r)
                if r + 1 < n_val - 1:
                    line_do("start", item, sign, r + 1)

    def split_c(block, k):
        rows = pl.ds(pl.multiple_of(block * cr, cr), cr)
        high, low = split(cf[block, k])
        ch[rows, columns(k)] = high
        cl[rows, columns(k)] = low

    def arrive(r, k):
        for sign in (1, -1):
            line_do("recv", c_item(k), sign, r)
            if r + 1 < n_val - 1:
                line_do("start", c_item(k), sign, r + 1)
        for sign in (1, -1):
            block, ok = line_block(sign, r, False)

            @pl.when(ok)
            def _():
                split_c(block, k)

    def split_own(k, carry):
        split_c(j, k)
        return carry

    def split_v(o, carry):
        rows = pl.ds(pl.multiple_of(o * vr, vr), vr)
        for t in range(n_pts):
            high, low = split(vf[t, rows])
            vh[rows, t * cw:(t + 1) * cw] = high
            vl[rows, t * cw:(t + 1) * cw] = low
        return carry

    def split_x(row0, size):
        rows = pl.ds(row0, size)
        for b in range(n_pts):
            high, low = split(xf[b, rows])
            xh[rows, b * cw:(b + 1) * cw] = high
            xl[rows, b * cw:(b + 1) * cw] = low

    def split_rows(t, carry):
        split_x(pl.multiple_of(t * ck, ck), ck)
        return carry

    for sign in (1, -1):
        line_do("start", x_item, sign, 0, x_ref)
        line_do("start", e_item, sign, 0, e_ref)
    unsent = list(range(nk))
    heads = list(range(nk)) if n_val > 2 else []
    send_c(unsent.pop(0))
    wait(own)
    start(gather_link(v_block, 0, vr, 0, 0, vls, vlr))
    for r in range(n_val - 1):
        x_round(r)
        for k in unsent[: 1 if r < n_val - 3 else nk]:
            send_c(k)
        unsent = unsent[1:] if r < n_val - 3 else []
        if r == 0:
            for step in range(1, m):
                wait(gather_link(v_block, 0, vr, step - 1, 0, vls, vlr))
                start(gather_link(v_block, 0, vr, step, 0, vls, vlr))
            wait(mine)
            lax.fori_loop(0, nk, split_own, 0)
        if 0 < r < n_val - 2 or n_val == 2:
            wait(gather_link(v_block, 0, vr, m - 1, 0, vls, vlr))
            start(gather_near(v_block, 0, vr, 0, vcs, vcr))
            if heads:
                arrive(0, heads.pop(0))
            wait(gather_near(v_block, 0, vr, 0, vcs, vcr))
            lax.fori_loop(0, n_pts, split_v, 0)
            if heads:
                arrive(0, heads.pop(0))
    first[0].wait()
    start(gather_link(x_block, 0, nv, 0, 0, als, alr))
    for step in range(1, m):
        wait(gather_link(x_block, 0, nv, step - 1, 0, als, alr))
        start(gather_link(x_block, 0, nv, step, 0, als, alr))
        if heads:
            arrive(0, heads.pop(0))
    wait(gather_link(x_block, 0, nv, m - 1, 0, als, alr))
    start(gather_near(x_block, 0, nv, 0, acs, acr))
    for k in heads:
        arrive(0, k)
    wait(gather_near(x_block, 0, nv, 0, acs, acr))
    lax.fori_loop(0, chunks, split_rows, 0)
    for r in range(n_val - 1):
        for sign in (1, -1):
            for item in (x_item, e_item):
                line_do("send", item, sign, r, x_ref if item is x_item else e_ref)
    wait(first[1:])

    def pass_on(r):
        def body(k, carry):
            arrive(r, k)
            return carry

        lax.fori_loop(0, nk, body, 0)

    for r in range(1, n_val - 2):
        pass_on(r)

    nt = min(512, nn)

    def store(high, low, at, value):
        a, b = split(value)
        high[at] = a
        low[at] = b

    def column(k, carry):
        arrive(n_val - 2, k)
        cols = columns(k)

        def pair(t, c):
            rows = pl.ds(pl.multiple_of(t * gr, gr), gr)
            store(ph, pl_, (rows, cols), product(
                ((1,), (0,)), (xh[rows], xl[rows]), (ch[:, cols], cl[:, cols])))
            return c

        lax.fori_loop(0, groups, pair, 0)

        def mixed(t, c):
            at = pl.ds(pl.multiple_of(t * nt, nt), nt)
            value = product(((0,), (0,)), (vh[:, at], vl[:, at]), (ph[:, cols], pl_[:, cols]))
            store(zh, zl, (at, cols), value * wf[at, cols])
            return c

        lax.fori_loop(0, nn // nt, mixed, 0)

        def back(t, c):
            rows = pl.ds(pl.multiple_of(t * gr, gr), gr)
            store(ph, pl_, (rows, cols), product(
                ((1,), (0,)), (vh[rows], vl[rows]), (zh[:, cols], zl[:, cols])))
            return c

        lax.fori_loop(0, groups, back, 0)
        return carry

    lax.fori_loop(0, nk, column, 0)

    def sent(k, carry):
        for r in range(n_val - 1):
            for sign in (1, -1):
                line_do("send", c_item(k), sign, r, c_ref.at[:, pl.ds(0, qc)])
        return carry

    lax.fori_loop(0, nk, sent, 0)

    def direct(g, flip):
        rows = pl.ds(g * gr, gr)

        def body(i, c):
            owner = p ^ flip ^ (2 * i)
            at = pl.ds(pl.multiple_of(owner * cw, cw), cw)
            df[owner, rows] = product(
                ((1,), (1,)), (ph[rows], pl_[rows]), (ch[at], cl[at]))
            return c

        lax.fori_loop(0, n_pts // 2, body, 0)

    def reduce_stages(c):
        stages = [lambda: (wait(reduce_near(c)), add_near(c), start(reduce_link(c, m - 1)))]
        for step in range(m - 1, 0, -1):
            stages.append(lambda step=step: (
                wait(reduce_link(c, step)), add_link(c, step), start(reduce_link(c, step - 1))))
        return stages

    def last_add(c):
        wait(reduce_link(c, 0))
        add_link(c, 0)

    def own_sum(c):
        rows = pl.ds(c * ck, ck)
        return df[p, rows]

    def scaled(c, newer, total):
        row0 = c % SUB * ck
        ediff = cond_ref[...] - ef[c // SUB].T[row0:row0 + ck, 0:1]
        hamil = ediff * newer - total
        return (hamil - CENTER * newer) / HALF_WIDTH

    def spread_stages(c):
        rows = pl.ds(c * ck, ck)
        stages = reduce_stages(c)
        source = df.at[p, rows]

        def to_inner():
            return remote(source, zin.at[rows], hs.at[c, 0], hr.at[c, 0], val=inner)

        def across():
            return remote(source, zx.at[rows], hs.at[c, 0], hr.at[c, 1], val=inner)

        def to_outer():
            return remote(zx.at[rows], zx.at[rows], hs.at[c, 1], hr.at[c, 1], val=outer)

        def inward(i):
            if i == 0:
                last_add(c)

            @pl.when(depth == i)
            def _():
                if i > 0:
                    to_inner().wait_recv()
                    df[p, rows] = df[p, rows] + zin[rows]
                (across() if i == half - 1 else to_inner()).start()

        def outward(i):
            @pl.when(depth == i)
            def _():
                across().wait_recv()
                if i == half - 1:
                    zx[rows] = zx[rows] + df[p, rows]
                if i > 0:
                    to_outer().start()

        def following():
            across().wait_send()

            @pl.when(depth > 0)
            def _():
                to_outer().wait_send()

            newer = xf[p, rows]
            xf[p, rows] = scaled(c, newer, zx[rows])
            start(gather_link(x_block, c * ck, ck, 0, c, als, alr))

        for i in range(half):
            stages.append(lambda i=i: inward(i))
        for i in range(half - 1, 0, -1):
            stages.append(lambda i=i: outward(i))
        stages.append(lambda: (outward(0), following()))
        for step in range(1, m):
            stages.append(lambda step=step: (
                wait(gather_link(x_block, c * ck, ck, step - 1, c, als, alr)),
                start(gather_link(x_block, c * ck, ck, step, c, als, alr))))
        stages.append(lambda: (
            wait(gather_link(x_block, c * ck, ck, m - 1, c, als, alr)),
            start(gather_near(x_block, c * ck, ck, c, acs, acr))))
        stages.append(lambda: (
            wait(gather_near(x_block, c * ck, ck, c, acs, acr)), split_x(c * ck, ck)))
        return stages

    def final_stages(c):
        rows = pl.ds(c * ck, ck)
        owner, part = c // SUB, pl.ds(c % SUB * ck, ck)
        stages = reduce_stages(c)

        def right():
            return remote(df.at[p, rows], fin.at[rows], hs.at[c, 0], hr.at[c, 0],
                          val=jnp.minimum(j + 1, last))

        def left():
            return remote(df.at[p, rows], fx.at[rows], hs.at[c, 0], hr.at[c, 1],
                          val=jnp.maximum(j - 1, 0))

        def step(i):
            if i == 0:
                last_add(c)
            if i < owner:
                @pl.when(j == i)
                def _():
                    if i > 0:
                        right().wait_recv()
                        df[p, rows] = df[p, rows] + fin[rows]
                    right().start()
            if last - i > owner:
                @pl.when(j == last - i)
                def _():
                    if i > 0:
                        left().wait_recv()
                        df[p, rows] = df[p, rows] + fx[rows]
                    left().start()

        def finish():
            @pl.when(j == owner)
            def _():
                total = df[p, rows]
                if owner > 0:
                    right().wait_recv()
                    total = total + fin[rows]
                if owner < last:
                    left().wait_recv()
                    total = total + fx[rows]
                out_ref[part] = 2.0 * scaled(c, xf[p, rows], total) - xo[part]

            @pl.when(j != owner)
            def _():
                right().wait_send()

        for i in range(max(owner, last - owner)):
            stages.append(lambda i=i: step(i))
        stages.append(finish)
        return stages

    per = chunks // groups

    def reduction(stages_of, order, fillers, lag, gap):
        direct(0, 1)
        for c in order[:per]:
            start(reduce_near(c))
        direct(0, 0)
        todo = {c: (at if at < per else at + lag, stages_of(c)) for at, c in enumerate(order)}
        end = max(b + gap * (len(s) - 1) + 1 for b, s in todo.values())
        for tick in range(end):
            if tick in fillers:
                fillers[tick]()
            for c in order:
                b, stages = todo[c]
                at, rest = divmod(tick - b, gap)
                if rest == 0 and 0 <= at < len(stages):
                    stages[at]()

    def near_rest(order):
        for c in order[per:]:
            start(reduce_near(c))

    qt = min(512, q)

    def pair(g):
        rows = pl.ds(g * gr, gr)

        def body(t, c):
            at = pl.ds(pl.multiple_of(t * qt, qt), qt)
            store(ph, pl_, (rows, at), product(
                ((1,), (0,)), (xh[rows], xl[rows]), (ch[:, at], cl[:, at])))
            return c

        lax.fori_loop(0, q // qt, body, 0)

    order = list(range(chunks))
    full = per + GAP * (len(spread_stages(0)) - 1)
    reduction(spread_stages, order, {
        0: lambda: direct(1, 1), 1: lambda: near_rest(order), 2: lambda: direct(1, 0),
        full: lambda: pair(0)}, 0, GAP)
    pair(1)

    def mixed(t, c):
        at = pl.ds(pl.multiple_of((t // (q // qt)) * nt, nt), nt)
        cols = pl.ds(pl.multiple_of((t % (q // qt)) * qt, qt), qt)
        value = product(((0,), (0,)), (vh[:, at], vl[:, at]), (ph[:, cols], pl_[:, cols]))
        store(zh, zl, (at, cols), value * wf[at, cols])
        return c

    lax.fori_loop(0, (nn // nt) * (q // qt), mixed, 0)

    def back(g):
        def body(t, c):
            rows = pl.ds(g * gr, gr)
            at = pl.ds(pl.multiple_of(t * qt, qt), qt)
            store(ph, pl_, (rows, at), product(
                ((1,), (0,)), (vh[rows], vl[rows]), (zh[:, at], zl[:, at])))
            return c

        lax.fori_loop(0, q // qt, body, 0)

    back(0)
    order = order[:per] + order[per:][::-1]
    reduction(final_stages, order, {
        0: lambda: back(1), 1: lambda: direct(1, 1), 2: lambda: (near_rest(order), direct(1, 0))}, 0, GAP)


def fused(n_pts, n_val, vectors, eval_energy, cond_energy, val_orbitals, cond_orbitals, screened):
    vb, cw = vectors.shape[1:]
    vr, nn = val_orbitals.shape
    cr, q = cond_orbitals.shape
    nv, nc = vb * n_val, cw * n_pts
    nk = q // QC
    m = n_pts.bit_length() - 2
    f32, bf16 = jnp.float32, jnp.bfloat16
    links, chunks = (1 << m) - 1, n_val * SUB
    any_, dma = pl.BlockSpec(memory_space=pl.ANY), pltpu.SemaphoreType.DMA
    vmem = pl.BlockSpec(memory_space=pltpu.VMEM)
    buffers = [
        ((n_val, nk, cr, QC), f32), ((nc, q), bf16), ((nc, q), bf16), ((nn, q), f32),
        ((n_pts, nv, cw), f32), ((nv, nn), bf16), ((nv, nn), bf16),
        ((n_pts, nv, cw), f32), ((nv, nc), bf16), ((nv, nc), bf16),
        ((nv, q), bf16), ((nv, q), bf16), ((nn, q), bf16), ((nn, q), bf16),
        ((n_pts // 2, nv, cw), f32), ((links, nv, cw), f32),
        ((nv, cw), f32), ((nv, cw), f32), ((nv, cw), f32), ((nv, cw), f32), ((vb, cw), f32),
        ((n_val, 8, vb), f32),
    ]
    semaphores = [
        (4 + nk + n_pts,), (2, n_val - 1, nk), (2, n_val - 1, nk), (2, 2, n_val - 1), (2, 2, n_val - 1),
        (1, m, links), (1, m, links), (1, n_pts // 2), (1, n_pts // 2),
        (chunks, m, links), (chunks, m, links), (chunks, n_pts // 2), (chunks, n_pts // 2),
        (chunks, m, links), (chunks, m, links), (chunks, n_pts // 2), (chunks, n_pts // 2),
        (chunks, 2), (chunks, 2),
    ]
    out = pl.pallas_call(
        functools.partial(fused_kernel, n_pts, n_val),
        out_shape=jax.ShapeDtypeStruct((vb, cw), f32),
        in_specs=[any_, any_, vmem, any_, any_, any_],
        out_specs=vmem,
        scratch_shapes=[pltpu.VMEM(*b) for b in buffers] + [dma(s) for s in semaphores],
        compiler_params=pltpu.CompilerParams(
            collective_id=0, has_side_effects=True, vmem_limit_bytes=VMEM_BYTES
        ),
    )(
        vectors[0], jnp.broadcast_to(eval_energy[None], (8, vb)), cond_energy[None],
        val_orbitals, cond_orbitals, screened,
    )
    return out[None]


def fits(n_pts, n_val, vectors, val_orbitals, cond_orbitals):
    vb, cw = vectors.shape[1:]
    vr, nn = val_orbitals.shape
    cr, q = cond_orbitals.shape
    nv, nc = vb * n_val, cw * n_pts
    m = n_pts.bit_length() - 2
    if n_pts & (n_pts - 1) or m < 1 or n_val % 2 or n_val < 2:
        return False
    if nn != nc or vb % LANES:
        return False
    if cw % LANES or q % QC or nn % 512 or vb % (16 * m * SUB) or vr % (16 * m) or cr % 16:
        return False
    held = 8 * nc * q + 8 * nn * q + 8 * nv * nn + 4 * nv * nc + 4 * nv * q
    held += 4 * nv * nc * 3 // 2 + 4 * nv * cw * ((1 << m) + 3)
    return held <= VMEM_BYTES - 3 * 2**20


def solution(mesh):
    placed = (
        P(None, "val", "pts"),
        P("val"),
        P("pts"),
        P("pts", "val"),
        P("val", "pts"),
        P("val", "pts"),
    )
    n_pts, n_val = mesh.shape["pts"], mesh.shape["val"]

    def body(vectors, eval_energy, cond_energy, val_orbitals, cond_orbitals, screened):
        run = fused if fits(n_pts, n_val, vectors, val_orbitals, cond_orbitals) else per_device
        return run(
            n_pts, n_val, vectors, eval_energy, cond_energy, val_orbitals, cond_orbitals, screened
        )

    return jax.shard_map(
        body, mesh=mesh, in_specs=placed, out_specs=P(None, "val", "pts"), check_vma=False
    )
```

```python
import functools

import jax
import jax.numpy as jnp
from jax import lax
from jax.experimental import pallas as pl
from jax.experimental.pallas import tpu as pltpu
from jax.sharding import PartitionSpec as P

ITERS = 2
PIECES = 32
PIECES_AHEAD = 6

CENTER = 2.2
HALF_WIDTH = 2.0

LANES = 128
QC = 256
SERVED = 1
SUB = 2
GAP = 2
VMEM_BYTES = 67_043_328


def dot(dims, a, b):
    return lax.dot_general(
        a, b, (dims, ((), ())), precision=lax.Precision.HIGH, preferred_element_type=jnp.float32
    )


def line_kernel(axis, count, part_ref, out_ref, came, last, came_send, came_recv, last_send, last_recv):
    at = lax.axis_index(axis)
    half = count // 2
    left = at < half
    inner = jnp.where(left, at + 1, at - 1)
    outer = jnp.where(left, at - 1, at + 1)
    edge = (at == 0) | (at == count - 1)
    middle = (at == half - 1) | (at == half)
    pieces = part_ref.shape[0]

    def copy(source, target, send, recv, to):
        return pltpu.make_async_remote_copy(
            src_ref=source, dst_ref=target, send_sem=send, recv_sem=recv,
            device_id={axis: to}, device_id_type=pl.DeviceIdType.MESH,
        )

    def to_inner(t):
        return copy(out_ref.at[t], came.at[t], came_send.at[t], came_recv.at[t], inner)

    def across(t):
        return copy(out_ref.at[t], last.at[t], came_send.at[t], last_recv.at[t], inner)

    def to_outer(t):
        return copy(last.at[t], last.at[t], last_send.at[t], last_recv.at[t], outer)

    barrier = pltpu.get_barrier_semaphore()
    pl.semaphore_signal(barrier, inc=1, device_id={axis: inner}, device_id_type=pl.DeviceIdType.MESH)

    @pl.when(jnp.logical_not(edge))
    def _():
        pl.semaphore_signal(
            barrier, inc=1, device_id={axis: outer}, device_id_type=pl.DeviceIdType.MESH
        )
        pl.semaphore_wait(barrier, 2)

    @pl.when(edge)
    def _():
        pl.semaphore_wait(barrier, 1)

    def inward(t, carry):
        out_ref[t] = part_ref[t]

        @pl.when(jnp.logical_not(edge))
        def _():
            to_inner(t).wait_recv()
            out_ref[t] = part_ref[t] + came[t]

        @pl.when(middle)
        def _():
            across(t).start()

        @pl.when(jnp.logical_not(middle))
        def _():
            to_inner(t).start()

        return carry

    def outward(t, carry):
        across(t).wait_recv()

        @pl.when(middle)
        def _():
            last[t] = last[t] + out_ref[t]

        @pl.when(jnp.logical_not(edge))
        def _():
            to_outer(t).start()

        to_inner(t).wait_send()
        out_ref[t] = last[t]
        return carry

    def drain(t, carry):
        @pl.when(jnp.logical_not(edge))
        def _():
            to_outer(t).wait_send()

        return carry

    @pl.when(edge)
    def _():
        lax.fori_loop(0, pieces, inward, 0)
        lax.fori_loop(0, pieces, outward, 0)

    @pl.when(jnp.logical_not(edge))
    def _():
        def both(t, carry):
            inward(t, carry)
            return outward(t - PIECES_AHEAD, carry)

        lax.fori_loop(0, PIECES_AHEAD, inward, 0)
        lax.fori_loop(PIECES_AHEAD, pieces, both, 0)
        lax.fori_loop(pieces - PIECES_AHEAD, pieces, outward, 0)

    lax.fori_loop(0, pieces, drain, 0)


def line_sum(part, axis, count):
    if count == 1:
        return part
    if count % 2:
        return lax.psum(part, axis)
    rows, columns = part.shape
    cut = (PIECES, rows // PIECES, columns)
    total = pl.pallas_call(
        functools.partial(line_kernel, axis, count),
        out_shape=jax.ShapeDtypeStruct(cut, jnp.float32),
        in_specs=[pl.BlockSpec(memory_space=pltpu.VMEM)],
        out_specs=pl.BlockSpec(memory_space=pltpu.VMEM),
        scratch_shapes=[pltpu.VMEM(cut, jnp.float32)] * 2 + [pltpu.SemaphoreType.DMA((PIECES,))] * 4,
        compiler_params=pltpu.CompilerParams(collective_id=0, has_side_effects=True),
    )(part.reshape(cut))
    return total.reshape(part.shape)


def cube_sum(part, axis, count, order):
    at = lax.axis_index(axis)
    for bit in order:
        pairs = [(i, i ^ (1 << bit)) for i in range(count)]
        mine = (at >> bit) & 1
        rows = part.shape[0] // 2
        gone = lax.dynamic_slice_in_dim(part, (1 - mine) * rows, rows, 0)
        kept = lax.dynamic_slice_in_dim(part, mine * rows, rows, 0)
        part = kept + lax.ppermute(gone, axis, pairs)
    for bit in reversed(order):
        pairs = [(i, i ^ (1 << bit)) for i in range(count)]
        mine = (at >> bit) & 1
        got = lax.ppermute(part, axis, pairs)
        part = jnp.where(
            mine == 0, jnp.concatenate([part, got], 0), jnp.concatenate([got, part], 0)
        )
    return part


def plane_sum(part, axis, count):
    if count & (count - 1):
        return lax.psum(part, axis)
    bits = list(range(count.bit_length() - 1))
    other = bits[:1] + bits[1:][::-1]
    mid = part.shape[0] // 2
    return jnp.concatenate(
        [cube_sum(part[:mid], axis, count, bits), cube_sum(part[mid:], axis, count, other)], 0
    )


def per_device(
    n_pts, n_val, vectors, eval_energy, cond_energy, val_orbitals, cond_orbitals, screened
):
    bands, width = vectors.shape[1], vectors.shape[2]
    own = cond_orbitals.shape[0]
    per = own // width
    j, p = lax.axis_index("val"), lax.axis_index("pts")
    mine = (p // per) == j
    place = (p % per) * width

    val_whole = lax.all_gather(val_orbitals, "pts", axis=0, tiled=True)

    extra = jnp.stack([cond_energy, jnp.pad(eval_energy, (0, width - bands))])
    extra = jnp.pad(extra, ((0, 6), (0, 0)))
    held = lax.all_gather(jnp.concatenate([vectors[0], extra]), "val", axis=0)
    eval_whole = held[:, bands + 1, :bands].reshape(-1)
    rows = held[:, :bands].reshape(-1, width)
    valence = rows.shape[0]
    rows = jnp.concatenate([rows, jnp.pad(cond_energy[None], ((0, 16 * n_pts - 1), (0, 0)))])
    spread = lax.dynamic_update_slice(
        jnp.zeros((rows.shape[0], own), jnp.float32),
        jnp.where(mine, rows, 0.0),
        (jnp.zeros_like(place), place),
    )
    spread = plane_sum(spread, "pts", n_pts)
    older = newer = spread[:valence]
    ediff = spread[valence][None, :] - eval_whole[:, None]

    for step in range(ITERS):
        pair = line_sum(dot(((1,), (0,)), newer, cond_orbitals), "val", n_val)
        weighted = dot(((0,), (0,)), val_whole, pair) * screened
        back = line_sum(dot(((1,), (0,)), val_whole, weighted), "val", n_val)
        direct = dot(((1,), (1,)), back, cond_orbitals)
        direct = plane_sum(direct, "pts", n_pts)
        hamil = ediff * newer - direct
        scaled = (hamil - CENTER * newer) / HALF_WIDTH
        if step == 0:
            following = scaled
        else:
            following = 2.0 * scaled - older
        older = newer
        newer = following

    out = lax.dynamic_slice_in_dim(newer, place, width, 1)
    out = lax.psum_scatter(jnp.where(mine, out, 0.0), "val", scatter_dimension=0, tiled=True)
    return out[None]


def split(x):
    high = x.astype(jnp.bfloat16)
    return high, (x - high.astype(jnp.float32)).astype(jnp.bfloat16)


def product(dims, a, b):
    def one(left, right):
        return lax.dot_general(left, right, (dims, ((), ())), preferred_element_type=jnp.float32)

    return one(a[0], b[0]) + one(a[0], b[1]) + one(a[1], b[0])


def spans(bits):
    offsets = [0]
    for bit in bits:
        offsets = offsets + [offset | (1 << bit) for offset in offsets]
    return offsets


def served_columns(n_val):
    return SERVED if n_val > 2 else 0


def fused_kernel(
    n_pts, n_val,
    x_ref, e_ref, cond_ref, v_ref, c_ref, w_ref, out_ref,
    cf, ch, cl, wf, vf, vh, vl, xf, xh, xl, ph, pl_, zh, zl, near, far, zin, zx, fin, fx, xo, ef, pbuf, bbuf,
    local, zs, zr, zsx, zrx, vls, vlr, vcs, vcr, als, alr, acs, acr, rls, rlr, rcs, rcr, hs, hr, ps, pr, bs, br, ds, dr,
):
    p, j = lax.axis_index("pts"), lax.axis_index("val")
    MESH = pl.DeviceIdType.MESH
    last = n_val - 1
    half = n_val // 2
    depth = jnp.minimum(j, last - j)
    inner = jnp.where(j < half, j + 1, j - 1)
    outer = jnp.clip(jnp.where(j < half, j - 1, j + 1), 0, last)
    nb = served_columns(n_val)
    bits = list(range(1, n_pts.bit_length() - 1))
    m = len(bits)
    orders = [bits[a:] + bits[:a] for a in range(m)]
    df = vf
    nv, cw = df.shape[1], df.shape[2]
    vb = nv // n_val
    ck = vb // SUB
    chunks = n_val * SUB
    nk, cr, qc = cf.shape[1], cf.shape[2], cf.shape[3]
    nn, q = wf.shape
    nc = ch.shape[0]
    vr = nv // n_pts
    groups = 2
    gr = nv // groups
    near_owners = [i << 1 for i in range(n_pts // 2)]

    def remote(source, target, send, recv, **to):
        return pltpu.make_async_remote_copy(
            src_ref=source, dst_ref=target, send_sem=send, recv_sem=recv,
            device_id=to, device_id_type=MESH,
        )

    def start(copies):
        for copy in copies:
            copy.start()

    def wait(copies):
        for copy in copies:
            copy.wait()

    def x_block(owner, row0, size):
        return xf.at[owner, pl.ds(row0, size)]

    def v_block(owner, row0, size):
        return vf.at[:, pl.ds(pl.multiple_of(owner * vr + row0, size), size)]

    def gather_link(block_of, row0, size, step, ident, send, recv):
        out = []
        for a, order in enumerate(orders):
            for i, d in enumerate(spans(order[:step])):
                at = (1 << step) - 1 + i
                block = block_of(p ^ d, row0 + a * (size // m), size // m)
                out.append(remote(block, block, send.at[ident, a, at], recv.at[ident, a, at],
                                  pts=p ^ (1 << order[step])))
        return out

    def gather_near(block_of, row0, size, ident, send, recv):
        out = []
        for i, d in enumerate(near_owners):
            block = block_of(p ^ d, row0, size)
            out.append(remote(block, block, send.at[ident, i], recv.at[ident, i], pts=p ^ 1))
        return out

    def reduce_near(c):
        rows = pl.ds(c * ck, ck)
        return [
            remote(df.at[p ^ 1 ^ d, rows], near.at[i, rows], rcs.at[c, i], rcr.at[c, i], pts=p ^ 1)
            for i, d in enumerate(near_owners)
        ]

    def reduce_link(c, step):
        out = []
        for a, order in enumerate(orders):
            rows = pl.ds(c * ck + a * (ck // m), ck // m)
            to = p ^ (1 << order[step])
            for i, d in enumerate(spans(order[:step])):
                at = (1 << step) - 1 + i
                out.append(remote(df.at[to ^ d, rows], far.at[at, rows], rls.at[c, a, at],
                                  rlr.at[c, a, at], pts=to))
        return out

    def add_near(c):
        rows = pl.ds(c * ck, ck)
        for i, d in enumerate(near_owners):
            df[p ^ d, rows] = df[p ^ d, rows] + near[i, rows]

    def add_link(c, step):
        for a, order in enumerate(orders):
            rows = pl.ds(c * ck + a * (ck // m), ck // m)
            for i, d in enumerate(spans(order[:step])):
                at = (1 << step) - 1 + i
                df[p ^ d, rows] = df[p ^ d, rows] + far[at, rows]

    def line_block(sign, r, sending):
        if sign > 0:
            block = j - r if sending else j - 1 - r
            edge = (j < last) if sending else (j > 0)
            ok = edge & (block >= 0)
        else:
            block = j + r if sending else j + 1 + r
            edge = (j > 0) if sending else (j < last)
            ok = edge & (block <= last)
        return jnp.clip(block, 0, last), ok

    def line_copy(item, sign, r, sending, first=None):
        block, ok = line_block(sign, r, sending)
        target, send, recv = item(block, 0 if sign > 0 else 1, r)
        source = first if (first is not None and r == 0 and sending) else target
        to = jnp.clip(j + sign, 0, last)
        return remote(source, target, send, recv, val=to), ok

    def x_item(block, way, r):
        return xf.at[p, pl.ds(block * vb, vb)], zsx.at[0, way, r], zrx.at[0, way, r]

    def e_item(block, way, r):
        return ef.at[block], zsx.at[1, way, r], zrx.at[1, way, r]

    def c_item(k):
        def item(block, way, r):
            return cf.at[block, k], zs.at[way, r, k], zr.at[way, r, k]

        return item

    def wanted(k, sign, sending):
        to = j + sign if sending else j
        return (k >= nb) | ((to > 0) & (to < last))

    def line_do(what, item, sign, r, first=None, k=None):
        copy, ok = line_copy(item, sign, r, what != "recv", first)
        if k is not None and nb:
            ok = ok & wanted(k, sign, what != "recv")

        @pl.when(ok)
        def _():
            if what == "start":
                copy.start()
            elif what == "recv":
                copy.wait_recv()
            else:
                copy.wait_send()

    def columns(k):
        return pl.ds(pl.multiple_of(k * qc, qc), qc)

    own = [
        pltpu.make_async_copy(v_ref.at[:, pl.ds(t * cw, cw)], vf.at[t, pl.ds(p * vr, vr)],
                              local.at[4 + nk + t])
        for t in range(n_pts)
    ]
    first = [
        pltpu.make_async_copy(x_ref, xf.at[p, pl.ds(j * vb, vb)], local.at[0]),
        pltpu.make_async_copy(e_ref, ef.at[j], local.at[1]),
        pltpu.make_async_copy(x_ref, xo, local.at[2]),
        pltpu.make_async_copy(w_ref, wf, local.at[3]),
    ]
    mine = [
        pltpu.make_async_copy(c_ref.at[:, pl.ds(k * qc, qc)], cf.at[j, k], local.at[4 + k])
        for k in range(nk)
    ]
    start(own)
    start(first[:3])
    start(mine)
    start(first[3:])

    barrier = pltpu.get_barrier_semaphore()
    for bit in [0] + bits:
        pl.semaphore_signal(barrier, inc=1, device_id={"pts": p ^ (1 << bit)}, device_id_type=MESH)

    @pl.when(j > 0)
    def _():
        pl.semaphore_signal(barrier, inc=1, device_id={"val": j - 1}, device_id_type=MESH)

    @pl.when(j < last)
    def _():
        pl.semaphore_signal(barrier, inc=1, device_id={"val": j + 1}, device_id_type=MESH)

    @pl.when(depth == 0)
    def _():
        pl.semaphore_wait(barrier, m + 2)

    @pl.when(depth > 0)
    def _():
        pl.semaphore_wait(barrier, m + 3)

    def send_c(k):
        for sign in (1, -1):
            line_do("start", c_item(k), sign, 0, c_ref.at[:, pl.ds(k * qc, qc)], k)

    def x_round(r):
        for sign in (1, -1):
            for item in (x_item, e_item):
                line_do("recv", item, sign, r)
                if r + 1 < n_val - 1:
                    line_do("start", item, sign, r + 1)

    def split_c(block, k):
        rows = pl.ds(pl.multiple_of(block * cr, cr), cr)
        high, low = split(cf[block, k])
        ch[rows, columns(k)] = high
        cl[rows, columns(k)] = low

    def arrive(r, k):
        for sign in (1, -1):
            line_do("recv", c_item(k), sign, r, None, k)
            if r + 1 < n_val - 1:
                line_do("start", c_item(k), sign, r + 1, None, k)
        for sign in (1, -1):
            block, ok = line_block(sign, r, False)
            if nb:
                ok = ok & wanted(k, sign, False)

            @pl.when(ok)
            def _():
                split_c(block, k)

    def split_own(k, carry):
        split_c(j, k)
        return carry

    def split_v(o, carry):
        rows = pl.ds(pl.multiple_of(o * vr, vr), vr)
        for t in range(n_pts):
            high, low = split(vf[t, rows])
            vh[rows, t * cw:(t + 1) * cw] = high
            vl[rows, t * cw:(t + 1) * cw] = low
        return carry

    def split_x(row0, size):
        rows = pl.ds(row0, size)
        for b in range(n_pts):
            high, low = split(xf[b, rows])
            xh[rows, b * cw:(b + 1) * cw] = high
            xl[rows, b * cw:(b + 1) * cw] = low

    def split_rows(t, carry):
        split_x(pl.multiple_of(t * ck, ck), ck)
        return carry

    def clear(t, carry):
        rows = pl.ds(pl.multiple_of(t * cr, cr), cr)
        for ref in (ch, cl):
            ref[rows, :nb * qc] = jnp.zeros((cr, nb * qc), jnp.bfloat16)
        return carry

    for sign in (1, -1):
        line_do("start", x_item, sign, 0, x_ref)
        line_do("start", e_item, sign, 0, e_ref)
    unsent = list(range(nk))
    heads = list(range(nk)) if n_val > 2 else []
    send_c(unsent.pop(0))
    wait(own)
    start(gather_link(v_block, 0, vr, 0, 0, vls, vlr))
    for r in range(n_val - 1):
        x_round(r)
        for k in unsent[: 1 if r < n_val - 3 else nk]:
            send_c(k)
        unsent = unsent[1:] if r < n_val - 3 else []
        if r == 0:
            for step in range(1, m):
                wait(gather_link(v_block, 0, vr, step - 1, 0, vls, vlr))
                start(gather_link(v_block, 0, vr, step, 0, vls, vlr))
            wait(mine)
            if nb:
                @pl.when(depth == 0)
                def _():
                    lax.fori_loop(0, nc // cr, clear, 0)

            first_split = jnp.where(depth == 0, nb, 0)
            lax.fori_loop(first_split, nk, split_own, 0)
        if 0 < r < n_val - 2 or n_val == 2:
            wait(gather_link(v_block, 0, vr, m - 1, 0, vls, vlr))
            start(gather_near(v_block, 0, vr, 0, vcs, vcr))
            if heads:
                arrive(0, heads.pop(0))
            wait(gather_near(v_block, 0, vr, 0, vcs, vcr))
            lax.fori_loop(0, n_pts, split_v, 0)
            if heads:
                arrive(0, heads.pop(0))
    first[0].wait()
    start(gather_link(x_block, 0, nv, 0, 0, als, alr))
    for step in range(1, m):
        wait(gather_link(x_block, 0, nv, step - 1, 0, als, alr))
        start(gather_link(x_block, 0, nv, step, 0, als, alr))
        if heads:
            arrive(0, heads.pop(0))
    wait(gather_link(x_block, 0, nv, m - 1, 0, als, alr))
    start(gather_near(x_block, 0, nv, 0, acs, acr))
    for k in heads:
        arrive(0, k)
    wait(gather_near(x_block, 0, nv, 0, acs, acr))
    lax.fori_loop(0, chunks, split_rows, 0)
    for r in range(n_val - 1):
        for sign in (1, -1):
            for item in (x_item, e_item):
                line_do("send", item, sign, r, x_ref if item is x_item else e_ref)
    wait(first[1:])

    nt = min(512, nn)

    def store(high, low, at, value):
        a, b = split(value)
        high[at] = a
        low[at] = b

    def group_rows(g):
        return pl.ds(pl.multiple_of(g * gr, gr), gr)

    def pass_p(slot, g):
        part = pbuf.at[slot, group_rows(g)]
        return remote(part, part, ps.at[slot, g], pr.at[slot, g], val=outer)

    def pass_b(slot, g):
        part = bbuf.at[slot, group_rows(g)]
        return remote(part, part, bs.at[slot, g], br.at[slot, g], val=inner)

    def late(k, i):
        block = jnp.where(j < half, i + 1, i)
        return block, remote(cf.at[block, k], cf.at[block, k], ds.at[k, i], dr.at[k, i], val=outer)

    def first_product(g, cols):
        rows = group_rows(g)
        return product(((1,), (0,)), (xh[rows], xl[rows]), (ch[:, cols], cl[:, cols]))

    def serve(k):
        def body(g, c):
            value = first_product(g, columns(k))
            pbuf[k, group_rows(g)] = value
            pass_p(k, g).start()
            store(ph, pl_, (group_rows(g), columns(k)), value)
            return c

        @pl.when(depth == 1)
        def _():
            lax.fori_loop(0, groups, body, 0)

    for r in range(1, n_val - 2):
        begin = nb if r == n_val - 3 else 0
        for k in range(begin):
            arrive(r, k)
            serve(k)

        def pass_on(k, carry):
            arrive(r, k)
            return carry

        lax.fori_loop(begin, nk, pass_on, 0)
    if nb:
        @pl.when(depth == 1)
        def _():
            for k in range(nb):
                for i in range(last):
                    late(k, i)[1].start()

    def column(turn, carry):
        k = jnp.where(depth == 0, turn, lax.rem(turn + nb, nk))
        arrive(n_val - 2, k)
        cols = columns(k)
        served = k < nb
        slot = jnp.minimum(k, max(nb - 1, 0))
        alone = jnp.logical_not(served & (depth <= 1))

        def pair(g, c):
            store(ph, pl_, (group_rows(g), cols), first_product(g, cols))
            return c

        @pl.when(alone)
        def _():
            lax.fori_loop(0, groups, pair, 0)

        if nb:
            def taken(g, c):
                pass_p(slot, g).wait_recv()
                store(ph, pl_, (group_rows(g), cols), pbuf[slot, group_rows(g)])
                return c

            @pl.when(served & (depth == 0))
            def _():
                lax.fori_loop(0, groups, taken, 0)

        def mixed(t, c):
            at = pl.ds(pl.multiple_of(t * nt, nt), nt)
            value = product(((0,), (0,)), (vh[:, at], vl[:, at]), (ph[:, cols], pl_[:, cols]))
            store(zh, zl, (at, cols), value * wf[at, cols])
            return c

        lax.fori_loop(0, nn // nt, mixed, 0)

        def back(g, c):
            rows = group_rows(g)
            value = product(((1,), (0,)), (vh[rows], vl[rows]), (zh[:, cols], zl[:, cols]))

            if nb:
                @pl.when(served & (depth == 0))
                def _():
                    bbuf[slot, rows] = value
                    pass_b(slot, g).start()
                    ph[rows, cols] = jnp.zeros((gr, qc), jnp.bfloat16)
                    pl_[rows, cols] = jnp.zeros((gr, qc), jnp.bfloat16)

                @pl.when(served & (depth == 1))
                def _():
                    pass_b(slot, g).wait_recv()
                    store(ph, pl_, (rows, cols), value + bbuf[slot, rows])

            @pl.when(alone)
            def _():
                store(ph, pl_, (rows, cols), value)

            return c

        lax.fori_loop(0, groups, back, 0)
        return carry

    lax.fori_loop(0, nk, column, 0)

    def sent(k, carry):
        for r in range(n_val - 1):
            for sign in (1, -1):
                line_do("send", c_item(k), sign, r, c_ref.at[:, pl.ds(0, qc)], k)
        return carry

    lax.fori_loop(0, nk, sent, 0)
    for k in range(nb):
        for g in range(groups):
            @pl.when(depth == 1)
            def _():
                pass_p(k, g).wait_send()

            @pl.when(depth == 0)
            def _():
                pass_b(k, g).wait_send()

    def late_end():
        for k in range(nb):
            @pl.when(depth == 0)
            def _():
                split_c(j, k)

            for i in range(last):
                @pl.when(depth == 1)
                def _():
                    late(k, i)[1].wait_send()

                @pl.when(depth == 0)
                def _():
                    block, copy = late(k, i)
                    copy.wait_recv()
                    split_c(block, k)

    def direct(g, flip):
        rows = pl.ds(g * gr, gr)

        def body(i, c):
            owner = p ^ flip ^ (2 * i)
            at = pl.ds(pl.multiple_of(owner * cw, cw), cw)
            df[owner, rows] = product(
                ((1,), (1,)), (ph[rows], pl_[rows]), (ch[at], cl[at]))
            return c

        lax.fori_loop(0, n_pts // 2, body, 0)

    def reduce_stages(c):
        stages = [lambda: (wait(reduce_near(c)), add_near(c), start(reduce_link(c, m - 1)))]
        for step in range(m - 1, 0, -1):
            stages.append(lambda step=step: (
                wait(reduce_link(c, step)), add_link(c, step), start(reduce_link(c, step - 1))))
        return stages

    def last_add(c):
        wait(reduce_link(c, 0))
        add_link(c, 0)

    def own_sum(c):
        rows = pl.ds(c * ck, ck)
        return df[p, rows]

    def scaled(c, newer, total):
        row0 = c % SUB * ck
        ediff = cond_ref[...] - ef[c // SUB].T[row0:row0 + ck, 0:1]
        hamil = ediff * newer - total
        return (hamil - CENTER * newer) / HALF_WIDTH

    def spread_stages(c):
        rows = pl.ds(c * ck, ck)
        stages = reduce_stages(c)
        source = df.at[p, rows]

        def to_inner():
            return remote(source, zin.at[rows], hs.at[c, 0], hr.at[c, 0], val=inner)

        def across():
            return remote(source, zx.at[rows], hs.at[c, 0], hr.at[c, 1], val=inner)

        def to_outer():
            return remote(zx.at[rows], zx.at[rows], hs.at[c, 1], hr.at[c, 1], val=outer)

        def inward(i):
            if i == 0:
                last_add(c)

            @pl.when(depth == i)
            def _():
                if i > 0:
                    to_inner().wait_recv()
                    df[p, rows] = df[p, rows] + zin[rows]
                (across() if i == half - 1 else to_inner()).start()

        def outward(i):
            @pl.when(depth == i)
            def _():
                across().wait_recv()
                if i == half - 1:
                    zx[rows] = zx[rows] + df[p, rows]
                if i > 0:
                    to_outer().start()

        def following():
            across().wait_send()

            @pl.when(depth > 0)
            def _():
                to_outer().wait_send()

            newer = xf[p, rows]
            xf[p, rows] = scaled(c, newer, zx[rows])
            start(gather_link(x_block, c * ck, ck, 0, c, als, alr))

        for i in range(half):
            stages.append(lambda i=i: inward(i))
        for i in range(half - 1, 0, -1):
            stages.append(lambda i=i: outward(i))
        stages.append(lambda: (outward(0), following()))
        for step in range(1, m):
            stages.append(lambda step=step: (
                wait(gather_link(x_block, c * ck, ck, step - 1, c, als, alr)),
                start(gather_link(x_block, c * ck, ck, step, c, als, alr))))
        stages.append(lambda: (
            wait(gather_link(x_block, c * ck, ck, m - 1, c, als, alr)),
            start(gather_near(x_block, c * ck, ck, c, acs, acr))))
        stages.append(lambda: (
            wait(gather_near(x_block, c * ck, ck, c, acs, acr)), split_x(c * ck, ck)))
        return stages

    def final_stages(c):
        rows = pl.ds(c * ck, ck)
        owner, part = c // SUB, pl.ds(c % SUB * ck, ck)
        stages = reduce_stages(c)

        def right():
            return remote(df.at[p, rows], fin.at[rows], hs.at[c, 0], hr.at[c, 0],
                          val=jnp.minimum(j + 1, last))

        def left():
            return remote(df.at[p, rows], fx.at[rows], hs.at[c, 0], hr.at[c, 1],
                          val=jnp.maximum(j - 1, 0))

        def step(i):
            if i == 0:
                last_add(c)
            if i < owner:
                @pl.when(j == i)
                def _():
                    if i > 0:
                        right().wait_recv()
                        df[p, rows] = df[p, rows] + fin[rows]
                    right().start()
            if last - i > owner:
                @pl.when(j == last - i)
                def _():
                    if i > 0:
                        left().wait_recv()
                        df[p, rows] = df[p, rows] + fx[rows]
                    left().start()

        def finish():
            @pl.when(j == owner)
            def _():
                total = df[p, rows]
                if owner > 0:
                    right().wait_recv()
                    total = total + fin[rows]
                if owner < last:
                    left().wait_recv()
                    total = total + fx[rows]
                out_ref[part] = 2.0 * scaled(c, xf[p, rows], total) - xo[part]

            @pl.when(j != owner)
            def _():
                right().wait_send()

        for i in range(max(owner, last - owner)):
            stages.append(lambda i=i: step(i))
        stages.append(finish)
        return stages

    per = chunks // groups

    def reduction(stages_of, order, fillers, lag, gap):
        direct(0, 1)
        for c in order[:per]:
            start(reduce_near(c))
        direct(0, 0)
        todo = {c: (at if at < per else at + lag, stages_of(c)) for at, c in enumerate(order)}
        end = max(b + gap * (len(s) - 1) + 1 for b, s in todo.values())
        for tick in range(end):
            if tick in fillers:
                fillers[tick]()
            for c in order:
                b, stages = todo[c]
                at, rest = divmod(tick - b, gap)
                if rest == 0 and 0 <= at < len(stages):
                    stages[at]()

    def near_rest(order):
        for c in order[per:]:
            start(reduce_near(c))

    qt = min(512, q)

    def pair(g):
        rows = pl.ds(g * gr, gr)

        def body(t, c):
            at = pl.ds(pl.multiple_of(t * qt, qt), qt)
            store(ph, pl_, (rows, at), product(
                ((1,), (0,)), (xh[rows], xl[rows]), (ch[:, at], cl[:, at])))
            return c

        lax.fori_loop(0, q // qt, body, 0)

    order = list(range(chunks))
    full = per + GAP * (len(spread_stages(0)) - 1)
    reduction(spread_stages, order, {
        0: lambda: direct(1, 1), 1: lambda: near_rest(order), 2: lambda: direct(1, 0),
        full: lambda: (late_end(), pair(0))}, 0, GAP)
    pair(1)

    def mixed(t, c):
        at = pl.ds(pl.multiple_of((t // (q // qt)) * nt, nt), nt)
        cols = pl.ds(pl.multiple_of((t % (q // qt)) * qt, qt), qt)
        value = product(((0,), (0,)), (vh[:, at], vl[:, at]), (ph[:, cols], pl_[:, cols]))
        store(zh, zl, (at, cols), value * wf[at, cols])
        return c

    lax.fori_loop(0, (nn // nt) * (q // qt), mixed, 0)

    def back(g):
        def body(t, c):
            rows = pl.ds(g * gr, gr)
            at = pl.ds(pl.multiple_of(t * qt, qt), qt)
            store(ph, pl_, (rows, at), product(
                ((1,), (0,)), (vh[rows], vl[rows]), (zh[:, at], zl[:, at])))
            return c

        lax.fori_loop(0, q // qt, body, 0)

    back(0)
    order = order[:per] + order[per:][::-1]
    reduction(final_stages, order, {
        0: lambda: back(1), 1: lambda: direct(1, 1), 2: lambda: (near_rest(order), direct(1, 0))}, 0, GAP)


def fused(n_pts, n_val, vectors, eval_energy, cond_energy, val_orbitals, cond_orbitals, screened):
    vb, cw = vectors.shape[1:]
    vr, nn = val_orbitals.shape
    cr, q = cond_orbitals.shape
    nv, nc = vb * n_val, cw * n_pts
    nk = q // QC
    m = n_pts.bit_length() - 2
    f32, bf16 = jnp.float32, jnp.bfloat16
    links, chunks = (1 << m) - 1, n_val * SUB
    kept = max(served_columns(n_val), 1)
    any_, dma = pl.BlockSpec(memory_space=pl.ANY), pltpu.SemaphoreType.DMA
    vmem = pl.BlockSpec(memory_space=pltpu.VMEM)
    buffers = [
        ((n_val, nk, cr, QC), f32), ((nc, q), bf16), ((nc, q), bf16), ((nn, q), f32),
        ((n_pts, nv, cw), f32), ((nv, nn), bf16), ((nv, nn), bf16),
        ((n_pts, nv, cw), f32), ((nv, nc), bf16), ((nv, nc), bf16),
        ((nv, q), bf16), ((nv, q), bf16), ((nn, q), bf16), ((nn, q), bf16),
        ((n_pts // 2, nv, cw), f32), ((links, nv, cw), f32),
        ((nv, cw), f32), ((nv, cw), f32), ((nv, cw), f32), ((nv, cw), f32), ((vb, cw), f32),
        ((n_val, 8, vb), f32), ((kept, nv, QC), f32), ((kept, nv, QC), f32),
    ]
    semaphores = [
        (4 + nk + n_pts,), (2, n_val - 1, nk), (2, n_val - 1, nk), (2, 2, n_val - 1), (2, 2, n_val - 1),
        (1, m, links), (1, m, links), (1, n_pts // 2), (1, n_pts // 2),
        (chunks, m, links), (chunks, m, links), (chunks, n_pts // 2), (chunks, n_pts // 2),
        (chunks, m, links), (chunks, m, links), (chunks, n_pts // 2), (chunks, n_pts // 2),
        (chunks, 2), (chunks, 2),
        (kept, 2), (kept, 2), (kept, 2), (kept, 2), (kept, n_val - 1), (kept, n_val - 1),
    ]
    out = pl.pallas_call(
        functools.partial(fused_kernel, n_pts, n_val),
        out_shape=jax.ShapeDtypeStruct((vb, cw), f32),
        in_specs=[any_, any_, vmem, any_, any_, any_],
        out_specs=vmem,
        scratch_shapes=[pltpu.VMEM(*b) for b in buffers] + [dma(s) for s in semaphores],
        compiler_params=pltpu.CompilerParams(
            collective_id=0, has_side_effects=True, vmem_limit_bytes=VMEM_BYTES
        ),
    )(
        vectors[0], jnp.broadcast_to(eval_energy[None], (8, vb)), cond_energy[None],
        val_orbitals, cond_orbitals, screened,
    )
    return out[None]


def fits(n_pts, n_val, vectors, val_orbitals, cond_orbitals):
    vb, cw = vectors.shape[1:]
    vr, nn = val_orbitals.shape
    cr, q = cond_orbitals.shape
    nv, nc = vb * n_val, cw * n_pts
    m = n_pts.bit_length() - 2
    if n_pts & (n_pts - 1) or m < 1 or n_val % 2 or n_val < 2:
        return False
    if nn != nc or vb % LANES:
        return False
    if q // QC <= served_columns(n_val):
        return False
    if cw % LANES or q % QC or nn % 512 or vb % (16 * m * SUB) or vr % (16 * m) or cr % 16:
        return False
    held = 8 * nc * q + 8 * nn * q + 8 * nv * nn + 4 * nv * nc + 4 * nv * q
    held += 4 * nv * nc * 3 // 2 + 4 * nv * cw * ((1 << m) + 3)
    held += 8 * nv * QC * served_columns(n_val)
    return held <= VMEM_BYTES - 3 * 2**20


def solution(mesh):
    placed = (
        P(None, "val", "pts"),
        P("val"),
        P("pts"),
        P("pts", "val"),
        P("val", "pts"),
        P("val", "pts"),
    )
    n_pts, n_val = mesh.shape["pts"], mesh.shape["val"]

    def body(vectors, eval_energy, cond_energy, val_orbitals, cond_orbitals, screened):
        run = fused if fits(n_pts, n_val, vectors, val_orbitals, cond_orbitals) else per_device
        return run(
            n_pts, n_val, vectors, eval_energy, cond_energy, val_orbitals, cond_orbitals, screened
        )

    return jax.shard_map(
        body, mesh=mesh, in_specs=placed, out_specs=P(None, "val", "pts"), check_vma=False
    )
```

```python
import functools

import jax
import jax.numpy as jnp
from jax import lax
from jax.experimental import pallas as pl
from jax.experimental.pallas import tpu as pltpu
from jax.sharding import PartitionSpec as P

ITERS = 2
PIECES = 32
PIECES_AHEAD = 6

CENTER = 2.2
HALF_WIDTH = 2.0

LANES = 128
QC = 256
SERVED = 1
LATE_NOW = 2
SUB = 2
GAP = 2
SPREAD = (0, 1, 0, 0.5)
FINAL = (0, 0.5, 0, 0.5)
FINAL_GAP = 2
VMEM_BYTES = 67_043_328


def dot(dims, a, b):
    return lax.dot_general(
        a, b, (dims, ((), ())), precision=lax.Precision.HIGH, preferred_element_type=jnp.float32
    )


def line_kernel(axis, count, part_ref, out_ref, came, last, came_send, came_recv, last_send, last_recv):
    at = lax.axis_index(axis)
    half = count // 2
    left = at < half
    inner = jnp.where(left, at + 1, at - 1)
    outer = jnp.where(left, at - 1, at + 1)
    edge = (at == 0) | (at == count - 1)
    middle = (at == half - 1) | (at == half)
    pieces = part_ref.shape[0]

    def copy(source, target, send, recv, to):
        return pltpu.make_async_remote_copy(
            src_ref=source, dst_ref=target, send_sem=send, recv_sem=recv,
            device_id={axis: to}, device_id_type=pl.DeviceIdType.MESH,
        )

    def to_inner(t):
        return copy(out_ref.at[t], came.at[t], came_send.at[t], came_recv.at[t], inner)

    def across(t):
        return copy(out_ref.at[t], last.at[t], came_send.at[t], last_recv.at[t], inner)

    def to_outer(t):
        return copy(last.at[t], last.at[t], last_send.at[t], last_recv.at[t], outer)

    barrier = pltpu.get_barrier_semaphore()
    pl.semaphore_signal(barrier, inc=1, device_id={axis: inner}, device_id_type=pl.DeviceIdType.MESH)

    @pl.when(jnp.logical_not(edge))
    def _():
        pl.semaphore_signal(
            barrier, inc=1, device_id={axis: outer}, device_id_type=pl.DeviceIdType.MESH
        )
        pl.semaphore_wait(barrier, 2)

    @pl.when(edge)
    def _():
        pl.semaphore_wait(barrier, 1)

    def inward(t, carry):
        out_ref[t] = part_ref[t]

        @pl.when(jnp.logical_not(edge))
        def _():
            to_inner(t).wait_recv()
            out_ref[t] = part_ref[t] + came[t]

        @pl.when(middle)
        def _():
            across(t).start()

        @pl.when(jnp.logical_not(middle))
        def _():
            to_inner(t).start()

        return carry

    def outward(t, carry):
        across(t).wait_recv()

        @pl.when(middle)
        def _():
            last[t] = last[t] + out_ref[t]

        @pl.when(jnp.logical_not(edge))
        def _():
            to_outer(t).start()

        to_inner(t).wait_send()
        out_ref[t] = last[t]
        return carry

    def drain(t, carry):
        @pl.when(jnp.logical_not(edge))
        def _():
            to_outer(t).wait_send()

        return carry

    @pl.when(edge)
    def _():
        lax.fori_loop(0, pieces, inward, 0)
        lax.fori_loop(0, pieces, outward, 0)

    @pl.when(jnp.logical_not(edge))
    def _():
        def both(t, carry):
            inward(t, carry)
            return outward(t - PIECES_AHEAD, carry)

        lax.fori_loop(0, PIECES_AHEAD, inward, 0)
        lax.fori_loop(PIECES_AHEAD, pieces, both, 0)
        lax.fori_loop(pieces - PIECES_AHEAD, pieces, outward, 0)

    lax.fori_loop(0, pieces, drain, 0)


def line_sum(part, axis, count):
    if count == 1:
        return part
    if count % 2:
        return lax.psum(part, axis)
    rows, columns = part.shape
    cut = (PIECES, rows // PIECES, columns)
    total = pl.pallas_call(
        functools.partial(line_kernel, axis, count),
        out_shape=jax.ShapeDtypeStruct(cut, jnp.float32),
        in_specs=[pl.BlockSpec(memory_space=pltpu.VMEM)],
        out_specs=pl.BlockSpec(memory_space=pltpu.VMEM),
        scratch_shapes=[pltpu.VMEM(cut, jnp.float32)] * 2 + [pltpu.SemaphoreType.DMA((PIECES,))] * 4,
        compiler_params=pltpu.CompilerParams(collective_id=0, has_side_effects=True),
    )(part.reshape(cut))
    return total.reshape(part.shape)


def cube_sum(part, axis, count, order):
    at = lax.axis_index(axis)
    for bit in order:
        pairs = [(i, i ^ (1 << bit)) for i in range(count)]
        mine = (at >> bit) & 1
        rows = part.shape[0] // 2
        gone = lax.dynamic_slice_in_dim(part, (1 - mine) * rows, rows, 0)
        kept = lax.dynamic_slice_in_dim(part, mine * rows, rows, 0)
        part = kept + lax.ppermute(gone, axis, pairs)
    for bit in reversed(order):
        pairs = [(i, i ^ (1 << bit)) for i in range(count)]
        mine = (at >> bit) & 1
        got = lax.ppermute(part, axis, pairs)
        part = jnp.where(
            mine == 0, jnp.concatenate([part, got], 0), jnp.concatenate([got, part], 0)
        )
    return part


def plane_sum(part, axis, count):
    if count & (count - 1):
        return lax.psum(part, axis)
    bits = list(range(count.bit_length() - 1))
    other = bits[:1] + bits[1:][::-1]
    mid = part.shape[0] // 2
    return jnp.concatenate(
        [cube_sum(part[:mid], axis, count, bits), cube_sum(part[mid:], axis, count, other)], 0
    )


def per_device(
    n_pts, n_val, vectors, eval_energy, cond_energy, val_orbitals, cond_orbitals, screened
):
    bands, width = vectors.shape[1], vectors.shape[2]
    own = cond_orbitals.shape[0]
    per = own // width
    j, p = lax.axis_index("val"), lax.axis_index("pts")
    mine = (p // per) == j
    place = (p % per) * width

    val_whole = lax.all_gather(val_orbitals, "pts", axis=0, tiled=True)

    extra = jnp.stack([cond_energy, jnp.pad(eval_energy, (0, width - bands))])
    extra = jnp.pad(extra, ((0, 6), (0, 0)))
    held = lax.all_gather(jnp.concatenate([vectors[0], extra]), "val", axis=0)
    eval_whole = held[:, bands + 1, :bands].reshape(-1)
    rows = held[:, :bands].reshape(-1, width)
    valence = rows.shape[0]
    rows = jnp.concatenate([rows, jnp.pad(cond_energy[None], ((0, 16 * n_pts - 1), (0, 0)))])
    spread = lax.dynamic_update_slice(
        jnp.zeros((rows.shape[0], own), jnp.float32),
        jnp.where(mine, rows, 0.0),
        (jnp.zeros_like(place), place),
    )
    spread = plane_sum(spread, "pts", n_pts)
    older = newer = spread[:valence]
    ediff = spread[valence][None, :] - eval_whole[:, None]

    for step in range(ITERS):
        pair = line_sum(dot(((1,), (0,)), newer, cond_orbitals), "val", n_val)
        weighted = dot(((0,), (0,)), val_whole, pair) * screened
        back = line_sum(dot(((1,), (0,)), val_whole, weighted), "val", n_val)
        direct = dot(((1,), (1,)), back, cond_orbitals)
        direct = plane_sum(direct, "pts", n_pts)
        hamil = ediff * newer - direct
        scaled = (hamil - CENTER * newer) / HALF_WIDTH
        if step == 0:
            following = scaled
        else:
            following = 2.0 * scaled - older
        older = newer
        newer = following

    out = lax.dynamic_slice_in_dim(newer, place, width, 1)
    out = lax.psum_scatter(jnp.where(mine, out, 0.0), "val", scatter_dimension=0, tiled=True)
    return out[None]


def split(x):
    high = x.astype(jnp.bfloat16)
    return high, (x - high.astype(jnp.float32)).astype(jnp.bfloat16)


def product(dims, a, b):
    def one(left, right):
        return lax.dot_general(left, right, (dims, ((), ())), preferred_element_type=jnp.float32)

    return one(a[0], b[0]) + one(a[0], b[1]) + one(a[1], b[0])


def spans(bits):
    offsets = [0]
    for bit in bits:
        offsets = offsets + [offset | (1 << bit) for offset in offsets]
    return offsets


def begin_ticks(chunks, form):
    early, pace, lag, rest = form
    per = chunks // 2
    out = [early + int(pace * i) for i in range(per)]
    return out + [max(out[-1] + 1, 3) + lag + int(rest * i) for i in range(per)]


def serves(n_val):
    return n_val > 2


def fused_kernel(
    n_pts, n_val,
    x_ref, e_ref, cond_ref, v_ref, c_ref, w_ref, out_ref,
    cf, ch, cl, wf, vf, vh, vl, xf, xh, xl, ph, pl_, zh, zl, near, far, zin, zx, fin, fx, xo, ef, pbuf, bbuf,
    local, zs, zr, zsx, zrx, vls, vlr, vcs, vcr, als, alr, acs, acr, rls, rlr, rcs, rcr, hs, hr, ps, pr, bs, br, ds, dr, fs, fr,
):
    p, j = lax.axis_index("pts"), lax.axis_index("val")
    MESH = pl.DeviceIdType.MESH
    last = n_val - 1
    half = n_val // 2
    depth = jnp.minimum(j, last - j)
    inner = jnp.where(j < half, j + 1, j - 1)
    outer = jnp.clip(jnp.where(j < half, j - 1, j + 1), 0, last)
    serving = serves(n_val)
    bits = list(range(1, n_pts.bit_length() - 1))
    m = len(bits)
    orders = [bits[a:] + bits[:a] for a in range(m)]
    df = vf
    nv, cw = df.shape[1], df.shape[2]
    vb = nv // n_val
    ck = vb // SUB
    chunks = n_val * SUB
    nk, cr, qc = cf.shape[1], cf.shape[2], cf.shape[3]
    nn, q = wf.shape
    nc = ch.shape[0]
    vr = nv // n_pts
    groups = 2
    gr = nv // groups
    near_owners = [i << 1 for i in range(n_pts // 2)]

    def remote(source, target, send, recv, **to):
        return pltpu.make_async_remote_copy(
            src_ref=source, dst_ref=target, send_sem=send, recv_sem=recv,
            device_id=to, device_id_type=MESH,
        )

    def start(copies):
        for copy in copies:
            copy.start()

    def wait(copies):
        for copy in copies:
            copy.wait()

    def x_block(owner, row0, size):
        return xf.at[owner, pl.ds(row0, size)]

    def v_block(owner, row0, size):
        return vf.at[:, pl.ds(pl.multiple_of(owner * vr + row0, size), size)]

    def gather_link(block_of, row0, size, step, ident, send, recv):
        out = []
        for a, order in enumerate(orders):
            for i, d in enumerate(spans(order[:step])):
                at = (1 << step) - 1 + i
                block = block_of(p ^ d, row0 + a * (size // m), size // m)
                out.append(remote(block, block, send.at[ident, a, at], recv.at[ident, a, at],
                                  pts=p ^ (1 << order[step])))
        return out

    def gather_near(block_of, row0, size, ident, send, recv):
        out = []
        for i, d in enumerate(near_owners):
            block = block_of(p ^ d, row0, size)
            out.append(remote(block, block, send.at[ident, i], recv.at[ident, i], pts=p ^ 1))
        return out

    def reduce_near(c):
        rows = pl.ds(c * ck, ck)
        return [
            remote(df.at[p ^ 1 ^ d, rows], near.at[i, rows], rcs.at[c, i], rcr.at[c, i], pts=p ^ 1)
            for i, d in enumerate(near_owners)
        ]

    def reduce_link(c, step):
        out = []
        for a, order in enumerate(orders):
            rows = pl.ds(c * ck + a * (ck // m), ck // m)
            to = p ^ (1 << order[step])
            for i, d in enumerate(spans(order[:step])):
                at = (1 << step) - 1 + i
                out.append(remote(df.at[to ^ d, rows], far.at[at, rows], rls.at[c, a, at],
                                  rlr.at[c, a, at], pts=to))
        return out

    def add_near(c):
        rows = pl.ds(c * ck, ck)
        for i, d in enumerate(near_owners):
            df[p ^ d, rows] = df[p ^ d, rows] + near[i, rows]

    def add_link(c, step):
        for a, order in enumerate(orders):
            rows = pl.ds(c * ck + a * (ck // m), ck // m)
            for i, d in enumerate(spans(order[:step])):
                at = (1 << step) - 1 + i
                df[p ^ d, rows] = df[p ^ d, rows] + far[at, rows]

    def line_block(sign, r, sending):
        if sign > 0:
            block = j - r if sending else j - 1 - r
            edge = (j < last) if sending else (j > 0)
            ok = edge & (block >= 0)
        else:
            block = j + r if sending else j + 1 + r
            edge = (j > 0) if sending else (j < last)
            ok = edge & (block <= last)
        return jnp.clip(block, 0, last), ok

    def line_copy(item, sign, r, sending, first=None):
        block, ok = line_block(sign, r, sending)
        target, send, recv = item(block, 0 if sign > 0 else 1, r)
        source = first if (first is not None and r == 0 and sending) else target
        to = jnp.clip(j + sign, 0, last)
        return remote(source, target, send, recv, val=to), ok

    def x_item(block, way, r):
        return xf.at[p, pl.ds(block * vb, vb)], zsx.at[0, way, r], zrx.at[0, way, r]

    def e_item(block, way, r):
        return ef.at[block], zsx.at[1, way, r], zrx.at[1, way, r]

    def c_item(k):
        def item(block, way, r):
            return cf.at[block, k], zs.at[way, r, k], zr.at[way, r, k]

        return item

    def wanted(k, sign, sending):
        to = j + sign if sending else j
        return (k != SERVED) | ((to > 0) & (to < last))

    def line_do(what, item, sign, r, first=None, k=None):
        copy, ok = line_copy(item, sign, r, what != "recv", first)
        if k is not None and serving:
            ok = ok & wanted(k, sign, what != "recv")

        @pl.when(ok)
        def _():
            if what == "start":
                copy.start()
            elif what == "recv":
                copy.wait_recv()
            else:
                copy.wait_send()

    def columns(k):
        return pl.ds(pl.multiple_of(k * qc, qc), qc)

    own = [
        pltpu.make_async_copy(v_ref.at[:, pl.ds(t * cw, cw)], vf.at[t, pl.ds(p * vr, vr)],
                              local.at[4 + nk + t])
        for t in range(n_pts)
    ]
    first = [
        pltpu.make_async_copy(x_ref, xf.at[p, pl.ds(j * vb, vb)], local.at[0]),
        pltpu.make_async_copy(x_ref, xo, local.at[1]),
        pltpu.make_async_copy(w_ref, wf, local.at[2]),
    ]
    mine = [
        pltpu.make_async_copy(c_ref.at[:, pl.ds(k * qc, qc)], cf.at[j, k], local.at[4 + k])
        for k in range(nk)
    ]
    start(own)
    start(first[:2])
    start(mine)
    start(first[2:])
    ef[j] = jnp.broadcast_to(e_ref[...], ef.shape[1:])

    barrier = pltpu.get_barrier_semaphore()
    for bit in [0] + bits:
        pl.semaphore_signal(barrier, inc=1, device_id={"pts": p ^ (1 << bit)}, device_id_type=MESH)

    @pl.when(j > 0)
    def _():
        pl.semaphore_signal(barrier, inc=1, device_id={"val": j - 1}, device_id_type=MESH)

    @pl.when(j < last)
    def _():
        pl.semaphore_signal(barrier, inc=1, device_id={"val": j + 1}, device_id_type=MESH)

    @pl.when(depth == 0)
    def _():
        pl.semaphore_wait(barrier, m + 2)

    @pl.when(depth > 0)
    def _():
        pl.semaphore_wait(barrier, m + 3)

    def send_c(k):
        for sign in (1, -1):
            line_do("start", c_item(k), sign, 0, c_ref.at[:, pl.ds(k * qc, qc)], k)

    def x_round(r):
        for sign in (1, -1):
            for item in (x_item, e_item):
                line_do("recv", item, sign, r)
                if r + 1 < n_val - 1:
                    line_do("start", item, sign, r + 1)

    def place(b):
        return b % 2 * (n_pts // 2) + b // 2

    def split_c(block, k):
        for i in range(cr // cw):
            rows = pl.ds(pl.multiple_of(place(block * (cr // cw) + i) * cw, cw), cw)
            high, low = split(cf[block, k, i * cw:(i + 1) * cw])
            ch[rows, columns(k)] = high
            cl[rows, columns(k)] = low

    def arrive(r, k):
        for sign in (1, -1):
            line_do("recv", c_item(k), sign, r, None, k)
            if r + 1 < n_val - 1:
                line_do("start", c_item(k), sign, r + 1, None, k)
        for sign in (1, -1):
            block, ok = line_block(sign, r, False)
            if serving:
                ok = ok & wanted(k, sign, False)

            @pl.when(ok)
            def _():
                split_c(block, k)

    def split_own(k, carry):
        split_c(j, k)
        return carry

    def split_v(o, carry):
        rows = pl.ds(pl.multiple_of(o * vr, vr), vr)
        for t in range(n_pts):
            high, low = split(vf[t, rows])
            vh[rows, t * cw:(t + 1) * cw] = high
            vl[rows, t * cw:(t + 1) * cw] = low
        return carry

    def split_x(row0, size):
        rows = pl.ds(row0, size)
        for b in range(n_pts):
            high, low = split(xf[b, rows])
            at = place(b) * cw
            xh[rows, at:at + cw] = high
            xl[rows, at:at + cw] = low

    def split_rows(t, carry):
        split_x(pl.multiple_of(t * ck, ck), ck)
        return carry

    def clear(t, carry):
        rows = pl.ds(pl.multiple_of(t * cr, cr), cr)
        for ref in (ch, cl):
            ref[rows, columns(SERVED)] = jnp.zeros((cr, qc), jnp.bfloat16)
        return carry

    for sign in (1, -1):
        line_do("start", x_item, sign, 0, x_ref)
        line_do("start", e_item, sign, 0)
    unsent = list(range(nk))
    heads = list(range(nk)) if n_val > 2 else []
    send_c(unsent.pop(0))
    wait(own)
    start(gather_link(v_block, 0, vr, 0, 0, vls, vlr))
    for r in range(n_val - 1):
        x_round(r)
        for k in unsent[: 1 if r < n_val - 3 else nk]:
            send_c(k)
        unsent = unsent[1:] if r < n_val - 3 else []
        if r == 0:
            for step in range(1, m):
                wait(gather_link(v_block, 0, vr, step - 1, 0, vls, vlr))
                start(gather_link(v_block, 0, vr, step, 0, vls, vlr))
            wait(mine)
            if serving:
                @pl.when(depth == 0)
                def _():
                    lax.fori_loop(0, nc // cr, clear, 0)

            lax.fori_loop(0, nk, split_own, 0)
        if 0 < r < n_val - 2 or n_val == 2:
            wait(gather_link(v_block, 0, vr, m - 1, 0, vls, vlr))
            start(gather_near(v_block, 0, vr, 0, vcs, vcr))
            if heads:
                arrive(0, heads.pop(0))
            wait(gather_near(v_block, 0, vr, 0, vcs, vcr))
            lax.fori_loop(0, n_pts, split_v, 0)
            if heads:
                arrive(0, heads.pop(0))
    first[0].wait()
    start(gather_link(x_block, 0, nv, 0, 0, als, alr))
    for step in range(1, m):
        wait(gather_link(x_block, 0, nv, step - 1, 0, als, alr))
        start(gather_link(x_block, 0, nv, step, 0, als, alr))
        if heads:
            arrive(0, heads.pop(0))
    wait(gather_link(x_block, 0, nv, m - 1, 0, als, alr))
    start(gather_near(x_block, 0, nv, 0, acs, acr))
    for k in heads:
        arrive(0, k)
    wait(gather_near(x_block, 0, nv, 0, acs, acr))
    lax.fori_loop(0, chunks, split_rows, 0)
    for r in range(n_val - 1):
        for sign in (1, -1):
            for item in (x_item, e_item):
                line_do("send", item, sign, r, x_ref if item is x_item else None)
    wait(first[1:])

    nt = min(512, nn)

    def store(high, low, at, value):
        a, b = split(value)
        high[at] = a
        low[at] = b

    def group_rows(g):
        return pl.ds(pl.multiple_of(g * gr, gr), gr)

    def pass_p(g):
        part = pbuf.at[group_rows(g)]
        return remote(part, part, ps.at[g], pr.at[g], val=outer)

    def pass_b(g):
        part = bbuf.at[group_rows(g)]
        return remote(part, part, bs.at[g], br.at[g], val=inner)

    def late(i):
        block = jnp.where(j < half, i + 1, i)
        part = cf.at[block, SERVED]
        return block, remote(part, part, ds.at[i], dr.at[i], val=outer)

    def first_product(g, cols):
        rows = group_rows(g)
        return product(((1,), (0,)), (xh[rows], xl[rows]), (ch[:, cols], cl[:, cols]))

    def serve(g, c):
        cols = columns(SERVED)
        value = first_product(g, cols)
        pbuf[group_rows(g)] = value
        pass_p(g).start()
        store(ph, pl_, (group_rows(g), cols), value)
        return c

    def column(k):
        cols = columns(k)
        served = (k == SERVED) if serving else (k < 0)
        alone = jnp.logical_not(served & (depth <= 1))

        def pair(g, c):
            store(ph, pl_, (group_rows(g), cols), first_product(g, cols))
            return c

        @pl.when(alone)
        def _():
            lax.fori_loop(0, groups, pair, 0)

        def taken(g, c):
            pass_p(g).wait_recv()
            store(ph, pl_, (group_rows(g), cols), pbuf[group_rows(g)])
            return c

        if serving:
            @pl.when(served & (depth == 0))
            def _():
                lax.fori_loop(0, groups, taken, 0)

        def mixed(t, c):
            at = pl.ds(pl.multiple_of(t * nt, nt), nt)
            value = product(((0,), (0,)), (vh[:, at], vl[:, at]), (ph[:, cols], pl_[:, cols]))
            store(zh, zl, (at, cols), value * wf[at, cols])
            return c

        lax.fori_loop(0, nn // nt, mixed, 0)

        def back(g, c):
            rows = group_rows(g)
            value = product(((1,), (0,)), (vh[rows], vl[rows]), (zh[:, cols], zl[:, cols]))

            if serving:
                @pl.when(served & (depth == 0))
                def _():
                    bbuf[rows] = value
                    pass_b(g).start()
                    ph[rows, cols] = jnp.zeros((gr, qc), jnp.bfloat16)
                    pl_[rows, cols] = jnp.zeros((gr, qc), jnp.bfloat16)

                @pl.when(served & (depth == 1))
                def _():
                    pass_b(g).wait_recv()
                    store(ph, pl_, (rows, cols), value + bbuf[rows])

            @pl.when(alone)
            def _():
                store(ph, pl_, (rows, cols), value)

            return c

        lax.fori_loop(0, groups, back, 0)

    for r in range(1, n_val - 2):
        def pass_on(k, carry):
            arrive(r, k)
            if r == n_val - 3:
                @pl.when((k == SERVED) & (depth == 1))
                def _():
                    lax.fori_loop(0, groups, serve, 0)

                @pl.when((k != SERVED) & (depth > 0))
                def _():
                    column(k)

            return carry

        lax.fori_loop(0, nk, pass_on, 0)

    def late_start(some):
        if serving:
            @pl.when(depth == 1)
            def _():
                for i in some:
                    late(i)[1].start()

    late_start(range(last)[:LATE_NOW])

    def finish_column(k, carry):
        arrive(n_val - 2, k)
        if serving:
            @pl.when((k == SERVED) | (depth == 0))
            def _():
                column(k)
        else:
            column(k)
        return carry

    lax.fori_loop(0, nk, finish_column, 0)

    def sent(k, carry):
        for r in range(n_val - 1):
            for sign in (1, -1):
                line_do("send", c_item(k), sign, r, c_ref.at[:, pl.ds(0, qc)], k)
        return carry

    lax.fori_loop(0, nk, sent, 0)
    if serving:
        for g in range(groups):
            @pl.when(depth == 1)
            def _():
                pass_p(g).wait_send()

            @pl.when(depth == 0)
            def _():
                pass_b(g).wait_send()

    def late_end():
        if not serving:
            return
        for i in range(last):
            @pl.when(depth == 1)
            def _():
                late(i)[1].wait_send()

            @pl.when(depth == 0)
            def _():
                block, copy = late(i)
                copy.wait_recv()
                split_c(block, SERVED)

    def direct(g, flip):
        rows = pl.ds(g * gr, gr)

        side = (p + flip) % 2

        def body(t, c):
            at = pl.ds(pl.multiple_of(side * (n_pts // 2 * cw) + t * (2 * cw), 2 * cw), 2 * cw)
            value = product(((1,), (1,)), (ph[rows], pl_[rows]), (ch[at], cl[at]))
            df[4 * t + side, rows] = value[:, :cw]
            df[4 * t + side + 2, rows] = value[:, cw:]
            return c

        lax.fori_loop(0, n_pts // 4, body, 0)

    def reduce_stages(c):
        stages = [lambda: (wait(reduce_near(c)), add_near(c), start(reduce_link(c, m - 1)))]
        for step in range(m - 1, 0, -1):
            stages.append(lambda step=step: (
                wait(reduce_link(c, step)), add_link(c, step), start(reduce_link(c, step - 1))))
        return stages

    def last_add(c):
        wait(reduce_link(c, 0))
        add_link(c, 0)

    def own_sum(c):
        rows = pl.ds(c * ck, ck)
        return df[p, rows]

    def scaled(c, newer, total):
        row0 = c % SUB * ck
        ediff = cond_ref[...] - ef[c // SUB].T[row0:row0 + ck, 0:1]
        hamil = ediff * newer - total
        return (hamil - CENTER * newer) / HALF_WIDTH

    def spread_stages(c):
        rows = pl.ds(c * ck, ck)
        stages = reduce_stages(c)
        source = df.at[p, rows]

        def to_inner():
            return remote(source, zin.at[rows], hs.at[c, 0], hr.at[c, 0], val=inner)

        def across():
            return remote(source, zx.at[rows], hs.at[c, 0], hr.at[c, 1], val=inner)

        def to_outer():
            return remote(zx.at[rows], zx.at[rows], hs.at[c, 1], hr.at[c, 1], val=outer)

        def inward(i):
            if i == 0:
                last_add(c)

            @pl.when(depth == i)
            def _():
                if i > 0:
                    to_inner().wait_recv()
                    df[p, rows] = df[p, rows] + zin[rows]
                (across() if i == half - 1 else to_inner()).start()

        def outward(i):
            @pl.when(depth == i)
            def _():
                across().wait_recv()
                if i == half - 1:
                    zx[rows] = zx[rows] + df[p, rows]
                if i > 0:
                    to_outer().start()

        def following():
            across().wait_send()

            @pl.when(depth > 0)
            def _():
                to_outer().wait_send()

            newer = xf[p, rows]
            xf[p, rows] = scaled(c, newer, zx[rows])
            start(gather_link(x_block, c * ck, ck, 0, c, als, alr))

        for i in range(half):
            stages.append(lambda i=i: inward(i))
        for i in range(half - 1, 0, -1):
            stages.append(lambda i=i: outward(i))
        stages.append(lambda: (outward(0), following()))
        for step in range(1, m):
            stages.append(lambda step=step: (
                wait(gather_link(x_block, c * ck, ck, step - 1, c, als, alr)),
                start(gather_link(x_block, c * ck, ck, step, c, als, alr))))
        stages.append(lambda: (
            wait(gather_link(x_block, c * ck, ck, m - 1, c, als, alr)),
            start(gather_near(x_block, c * ck, ck, c, acs, acr))))
        stages.append(lambda: (
            wait(gather_near(x_block, c * ck, ck, c, acs, acr)), split_x(c * ck, ck)))
        return stages

    def final_stages(c):
        rows = pl.ds(c * ck, ck)
        owner, part = c // SUB, pl.ds(c % SUB * ck, ck)
        stages = reduce_stages(c)

        def right():
            return remote(df.at[p, rows], fin.at[rows], fs.at[c, 0], fr.at[c, 0],
                          val=jnp.minimum(j + 1, last))

        def left():
            return remote(df.at[p, rows], fx.at[rows], fs.at[c, 0], fr.at[c, 1],
                          val=jnp.maximum(j - 1, 0))

        def step(i):
            if i == 0:
                last_add(c)
            if i < owner:
                @pl.when(j == i)
                def _():
                    if i > 0:
                        right().wait_recv()
                        df[p, rows] = df[p, rows] + fin[rows]
                    right().start()
            if last - i > owner:
                @pl.when(j == last - i)
                def _():
                    if i > 0:
                        left().wait_recv()
                        df[p, rows] = df[p, rows] + fx[rows]
                    left().start()

        def finish():
            @pl.when(j == owner)
            def _():
                total = df[p, rows]
                if owner > 0:
                    right().wait_recv()
                    total = total + fin[rows]
                if owner < last:
                    left().wait_recv()
                    total = total + fx[rows]
                out_ref[part] = 2.0 * scaled(c, xf[p, rows], total) - xo[part]

            @pl.when(j != owner)
            def _():
                right().wait_send()

        for i in range(max(owner, last - owner)):
            stages.append(lambda i=i: step(i))
        stages.append(finish)
        return stages

    per = chunks // groups

    def reduction(stages_of, order, fillers, begins, gap):
        direct(0, 1)
        for c in order[:per]:
            start(reduce_near(c))
        direct(0, 0)
        todo = {c: (begin, stages_of(c)) for begin, c in zip(begins, order)}
        end = max(b + gap * (len(s) - 1) + 1 for b, s in todo.values())
        for tick in range(end):
            if tick in fillers:
                fillers[tick]()
            for c in order:
                b, stages = todo[c]
                at, rest = divmod(tick - b, gap)
                if rest == 0 and 0 <= at < len(stages):
                    stages[at]()

    def near_rest(order):
        for c in order[per:]:
            start(reduce_near(c))

    qt = min(512, q)

    def pair(g, begin, end):
        rows = pl.ds(g * gr, gr)

        def body(t, c):
            at = pl.ds(pl.multiple_of(t * qt, qt), qt)
            store(ph, pl_, (rows, at), product(
                ((1,), (0,)), (xh[rows], xl[rows]), (ch[:, at], cl[:, at])))
            return c

        lax.fori_loop(begin, end, body, 0)

    order = list(range(chunks))
    begins = begin_ticks(chunks, SPREAD)
    stages = len(spread_stages(0))
    full = begins[per - 1] + GAP * (stages - 1) + 1
    freed = begins[-1] + GAP * (stages - 5) + 1
    fillers = {
        0: lambda: direct(1, 1), 1: lambda: near_rest(order), 2: lambda: direct(1, 0),
        freed: lambda: late_start(range(last)[LATE_NOW:]), full: lambda: pair(0, 1, q // qt)}
    reduction(spread_stages, order, fillers, begins, GAP)
    pair(1, 1, q // qt)
    late_end()
    pair(0, 0, 1)
    pair(1, 0, 1)

    def mixed(t, c):
        at = pl.ds(pl.multiple_of((t // (q // qt)) * nt, nt), nt)
        cols = pl.ds(pl.multiple_of((t % (q // qt)) * qt, qt), qt)
        value = product(((0,), (0,)), (vh[:, at], vl[:, at]), (ph[:, cols], pl_[:, cols]))
        store(zh, zl, (at, cols), value * wf[at, cols])
        return c

    lax.fori_loop(0, (nn // nt) * (q // qt), mixed, 0)

    def back(g):
        def body(t, c):
            rows = pl.ds(g * gr, gr)
            at = pl.ds(pl.multiple_of(t * qt, qt), qt)
            store(ph, pl_, (rows, at), product(
                ((1,), (0,)), (vh[rows], vl[rows]), (zh[:, at], zl[:, at])))
            return c

        lax.fori_loop(0, q // qt, body, 0)

    back(0)
    order = order[:per] + order[per:][::-1]
    reduction(final_stages, order, {
        0: lambda: back(1), 1: lambda: direct(1, 1), 2: lambda: (near_rest(order), direct(1, 0)),
    }, begin_ticks(chunks, FINAL), FINAL_GAP)


def fused(n_pts, n_val, vectors, eval_energy, cond_energy, val_orbitals, cond_orbitals, screened):
    vb, cw = vectors.shape[1:]
    vr, nn = val_orbitals.shape
    cr, q = cond_orbitals.shape
    nv, nc = vb * n_val, cw * n_pts
    nk = q // QC
    m = n_pts.bit_length() - 2
    f32, bf16 = jnp.float32, jnp.bfloat16
    links, chunks = (1 << m) - 1, n_val * SUB
    any_, dma = pl.BlockSpec(memory_space=pl.ANY), pltpu.SemaphoreType.DMA
    vmem = pl.BlockSpec(memory_space=pltpu.VMEM)
    buffers = [
        ((n_val, nk, cr, QC), f32), ((nc, q), bf16), ((nc, q), bf16), ((nn, q), f32),
        ((n_pts, nv, cw), f32), ((nv, nn), bf16), ((nv, nn), bf16),
        ((n_pts, nv, cw), f32), ((nv, nc), bf16), ((nv, nc), bf16),
        ((nv, q), bf16), ((nv, q), bf16), ((nn, q), bf16), ((nn, q), bf16),
        ((n_pts // 2, nv, cw), f32), ((links, nv, cw), f32),
        ((nv, cw), f32), ((nv, cw), f32), ((nv, cw), f32), ((nv, cw), f32), ((vb, cw), f32),
        ((n_val, 8, vb), f32), ((nv, QC), f32), ((nv, QC), f32),
    ]
    semaphores = [
        (4 + nk + n_pts,), (2, n_val - 1, nk), (2, n_val - 1, nk), (2, 2, n_val - 1), (2, 2, n_val - 1),
        (1, m, links), (1, m, links), (1, n_pts // 2), (1, n_pts // 2),
        (chunks, m, links), (chunks, m, links), (chunks, n_pts // 2), (chunks, n_pts // 2),
        (chunks, m, links), (chunks, m, links), (chunks, n_pts // 2), (chunks, n_pts // 2),
        (chunks, 2), (chunks, 2),
        (2,), (2,), (2,), (2,), (n_val - 1,), (n_val - 1,),
        (chunks, 2), (chunks, 2),
    ]
    out = pl.pallas_call(
        functools.partial(fused_kernel, n_pts, n_val),
        out_shape=jax.ShapeDtypeStruct((vb, cw), f32),
        in_specs=[any_, vmem, vmem, any_, any_, any_],
        out_specs=vmem,
        scratch_shapes=[pltpu.VMEM(*b) for b in buffers] + [dma(s) for s in semaphores],
        compiler_params=pltpu.CompilerParams(
            collective_id=0, has_side_effects=True, vmem_limit_bytes=VMEM_BYTES
        ),
    )(
        vectors[0], eval_energy[None], cond_energy[None],
        val_orbitals, cond_orbitals, screened,
    )
    return out[None]


def fits(n_pts, n_val, vectors, val_orbitals, cond_orbitals):
    vb, cw = vectors.shape[1:]
    vr, nn = val_orbitals.shape
    cr, q = cond_orbitals.shape
    nv, nc = vb * n_val, cw * n_pts
    m = n_pts.bit_length() - 2
    if n_pts & (n_pts - 1) or m < 1 or n_val % 2 or n_val < 2:
        return False
    if nn != nc or vb % LANES:
        return False
    if q // QC <= SERVED + 1:
        return False
    if cr % cw or (SERVED + 1) * QC > 512:
        return False
    if cw % LANES or q % QC or nn % 512 or vb % (16 * m * SUB) or vr % (16 * m) or cr % 16:
        return False
    held = 8 * nc * q + 8 * nn * q + 8 * nv * nn + 4 * nv * nc + 4 * nv * q
    held += 4 * nv * nc * 3 // 2 + 4 * nv * cw * ((1 << m) + 3)
    held += 8 * nv * QC
    return held <= VMEM_BYTES - 3 * 2**20


def solution(mesh):
    placed = (
        P(None, "val", "pts"),
        P("val"),
        P("pts"),
        P("pts", "val"),
        P("val", "pts"),
        P("val", "pts"),
    )
    n_pts, n_val = mesh.shape["pts"], mesh.shape["val"]

    def body(vectors, eval_energy, cond_energy, val_orbitals, cond_orbitals, screened):
        run = fused if fits(n_pts, n_val, vectors, val_orbitals, cond_orbitals) else per_device
        return run(
            n_pts, n_val, vectors, eval_energy, cond_energy, val_orbitals, cond_orbitals, screened
        )

    return jax.shard_map(
        body, mesh=mesh, in_specs=placed, out_specs=P(None, "val", "pts"), check_vma=False
    )
```

```python
import functools

import jax
import jax.numpy as jnp
from jax import lax
from jax.experimental import pallas as pl
from jax.experimental.pallas import tpu as pltpu
from jax.sharding import PartitionSpec as P

ITERS = 2
PIECES = 32
PIECES_AHEAD = 6

CENTER = 2.2
HALF_WIDTH = 2.0

LANES = 128
QC = 256
SERVED = 1
LATE_NOW = 2
SUB = 2
GAP = 2
SPREAD = (0, 1, 0, 0.5)
FINAL = (0, 0.5, 0, 0.5)
FINAL_GAP = 2
VMEM_BYTES = 67_043_328


def dot(dims, a, b):
    return lax.dot_general(
        a, b, (dims, ((), ())), precision=lax.Precision.HIGH, preferred_element_type=jnp.float32
    )


def line_kernel(axis, count, part_ref, out_ref, came, last, came_send, came_recv, last_send, last_recv):
    at = lax.axis_index(axis)
    half = count // 2
    left = at < half
    inner = jnp.where(left, at + 1, at - 1)
    outer = jnp.where(left, at - 1, at + 1)
    edge = (at == 0) | (at == count - 1)
    middle = (at == half - 1) | (at == half)
    pieces = part_ref.shape[0]

    def copy(source, target, send, recv, to):
        return pltpu.make_async_remote_copy(
            src_ref=source, dst_ref=target, send_sem=send, recv_sem=recv,
            device_id={axis: to}, device_id_type=pl.DeviceIdType.MESH,
        )

    def to_inner(t):
        return copy(out_ref.at[t], came.at[t], came_send.at[t], came_recv.at[t], inner)

    def across(t):
        return copy(out_ref.at[t], last.at[t], came_send.at[t], last_recv.at[t], inner)

    def to_outer(t):
        return copy(last.at[t], last.at[t], last_send.at[t], last_recv.at[t], outer)

    barrier = pltpu.get_barrier_semaphore()
    pl.semaphore_signal(barrier, inc=1, device_id={axis: inner}, device_id_type=pl.DeviceIdType.MESH)

    @pl.when(jnp.logical_not(edge))
    def _():
        pl.semaphore_signal(
            barrier, inc=1, device_id={axis: outer}, device_id_type=pl.DeviceIdType.MESH
        )
        pl.semaphore_wait(barrier, 2)

    @pl.when(edge)
    def _():
        pl.semaphore_wait(barrier, 1)

    def inward(t, carry):
        out_ref[t] = part_ref[t]

        @pl.when(jnp.logical_not(edge))
        def _():
            to_inner(t).wait_recv()
            out_ref[t] = part_ref[t] + came[t]

        @pl.when(middle)
        def _():
            across(t).start()

        @pl.when(jnp.logical_not(middle))
        def _():
            to_inner(t).start()

        return carry

    def outward(t, carry):
        across(t).wait_recv()

        @pl.when(middle)
        def _():
            last[t] = last[t] + out_ref[t]

        @pl.when(jnp.logical_not(edge))
        def _():
            to_outer(t).start()

        to_inner(t).wait_send()
        out_ref[t] = last[t]
        return carry

    def drain(t, carry):
        @pl.when(jnp.logical_not(edge))
        def _():
            to_outer(t).wait_send()

        return carry

    @pl.when(edge)
    def _():
        lax.fori_loop(0, pieces, inward, 0)
        lax.fori_loop(0, pieces, outward, 0)

    @pl.when(jnp.logical_not(edge))
    def _():
        def both(t, carry):
            inward(t, carry)
            return outward(t - PIECES_AHEAD, carry)

        lax.fori_loop(0, PIECES_AHEAD, inward, 0)
        lax.fori_loop(PIECES_AHEAD, pieces, both, 0)
        lax.fori_loop(pieces - PIECES_AHEAD, pieces, outward, 0)

    lax.fori_loop(0, pieces, drain, 0)


def line_sum(part, axis, count):
    if count == 1:
        return part
    if count % 2:
        return lax.psum(part, axis)
    rows, columns = part.shape
    cut = (PIECES, rows // PIECES, columns)
    total = pl.pallas_call(
        functools.partial(line_kernel, axis, count),
        out_shape=jax.ShapeDtypeStruct(cut, jnp.float32),
        in_specs=[pl.BlockSpec(memory_space=pltpu.VMEM)],
        out_specs=pl.BlockSpec(memory_space=pltpu.VMEM),
        scratch_shapes=[pltpu.VMEM(cut, jnp.float32)] * 2 + [pltpu.SemaphoreType.DMA((PIECES,))] * 4,
        compiler_params=pltpu.CompilerParams(collective_id=0, has_side_effects=True),
    )(part.reshape(cut))
    return total.reshape(part.shape)


def cube_sum(part, axis, count, order):
    at = lax.axis_index(axis)
    for bit in order:
        pairs = [(i, i ^ (1 << bit)) for i in range(count)]
        mine = (at >> bit) & 1
        rows = part.shape[0] // 2
        gone = lax.dynamic_slice_in_dim(part, (1 - mine) * rows, rows, 0)
        kept = lax.dynamic_slice_in_dim(part, mine * rows, rows, 0)
        part = kept + lax.ppermute(gone, axis, pairs)
    for bit in reversed(order):
        pairs = [(i, i ^ (1 << bit)) for i in range(count)]
        mine = (at >> bit) & 1
        got = lax.ppermute(part, axis, pairs)
        part = jnp.where(
            mine == 0, jnp.concatenate([part, got], 0), jnp.concatenate([got, part], 0)
        )
    return part


def plane_sum(part, axis, count):
    if count & (count - 1):
        return lax.psum(part, axis)
    bits = list(range(count.bit_length() - 1))
    other = bits[:1] + bits[1:][::-1]
    mid = part.shape[0] // 2
    return jnp.concatenate(
        [cube_sum(part[:mid], axis, count, bits), cube_sum(part[mid:], axis, count, other)], 0
    )


def per_device(
    n_pts, n_val, vectors, eval_energy, cond_energy, val_orbitals, cond_orbitals, screened
):
    bands, width = vectors.shape[1], vectors.shape[2]
    own = cond_orbitals.shape[0]
    per = own // width
    j, p = lax.axis_index("val"), lax.axis_index("pts")
    mine = (p // per) == j
    place = (p % per) * width

    val_whole = lax.all_gather(val_orbitals, "pts", axis=0, tiled=True)

    extra = jnp.stack([cond_energy, jnp.pad(eval_energy, (0, width - bands))])
    extra = jnp.pad(extra, ((0, 6), (0, 0)))
    held = lax.all_gather(jnp.concatenate([vectors[0], extra]), "val", axis=0)
    eval_whole = held[:, bands + 1, :bands].reshape(-1)
    rows = held[:, :bands].reshape(-1, width)
    valence = rows.shape[0]
    rows = jnp.concatenate([rows, jnp.pad(cond_energy[None], ((0, 16 * n_pts - 1), (0, 0)))])
    spread = lax.dynamic_update_slice(
        jnp.zeros((rows.shape[0], own), jnp.float32),
        jnp.where(mine, rows, 0.0),
        (jnp.zeros_like(place), place),
    )
    spread = plane_sum(spread, "pts", n_pts)
    older = newer = spread[:valence]
    ediff = spread[valence][None, :] - eval_whole[:, None]

    for step in range(ITERS):
        pair = line_sum(dot(((1,), (0,)), newer, cond_orbitals), "val", n_val)
        weighted = dot(((0,), (0,)), val_whole, pair) * screened
        back = line_sum(dot(((1,), (0,)), val_whole, weighted), "val", n_val)
        direct = dot(((1,), (1,)), back, cond_orbitals)
        direct = plane_sum(direct, "pts", n_pts)
        hamil = ediff * newer - direct
        scaled = (hamil - CENTER * newer) / HALF_WIDTH
        if step == 0:
            following = scaled
        else:
            following = 2.0 * scaled - older
        older = newer
        newer = following

    out = lax.dynamic_slice_in_dim(newer, place, width, 1)
    out = lax.psum_scatter(jnp.where(mine, out, 0.0), "val", scatter_dimension=0, tiled=True)
    return out[None]


def split(x):
    high = x.astype(jnp.bfloat16)
    return high, (x - high.astype(jnp.float32)).astype(jnp.bfloat16)


def product(dims, a, b):
    def one(left, right):
        return lax.dot_general(left, right, (dims, ((), ())), preferred_element_type=jnp.float32)

    return one(a[0], b[0]) + one(a[0], b[1]) + one(a[1], b[0])


def spans(bits):
    offsets = [0]
    for bit in bits:
        offsets = offsets + [offset | (1 << bit) for offset in offsets]
    return offsets


def begin_ticks(chunks, form):
    early, pace, lag, rest = form
    per = chunks // 2
    out = [early + int(pace * i) for i in range(per)]
    return out + [max(out[-1] + 1, 3) + lag + int(rest * i) for i in range(per)]


def serves(n_val):
    return n_val > 2


def fused_kernel(
    n_pts, n_val,
    x_ref, e_ref, cond_ref, v_ref, c_ref, w_ref, out_ref,
    cf, ch, cl, wf, vf, vh, vl, xf, xh, xl, ph, pl_, zh, zl, near, far, zin, zx, fin, fx, xo, ef, pbuf, bbuf,
    local, zs, zr, zsx, zrx, vls, vlr, vcs, vcr, als, alr, acs, acr, rls, rlr, rcs, rcr, hs, hr, ps, pr, bs, br, ds, dr, fs, fr,
):
    p, j = lax.axis_index("pts"), lax.axis_index("val")
    MESH = pl.DeviceIdType.MESH
    last = n_val - 1
    half = n_val // 2
    depth = jnp.minimum(j, last - j)
    inner = jnp.where(j < half, j + 1, j - 1)
    outer = jnp.clip(jnp.where(j < half, j - 1, j + 1), 0, last)
    serving = serves(n_val)
    bits = list(range(1, n_pts.bit_length() - 1))
    m = len(bits)
    orders = [bits[a:] + bits[:a] for a in range(m)]
    df = vf
    nv, cw = df.shape[1], df.shape[2]
    vb = nv // n_val
    ck = vb // SUB
    chunks = n_val * SUB
    nk, cr, qc = cf.shape[1], cf.shape[2], cf.shape[3]
    nn, q = wf.shape
    nc = ch.shape[0]
    vr = nv // n_pts
    groups = 2
    gr = nv // groups
    near_owners = [i << 1 for i in range(n_pts // 2)]

    def place(b):
        return b % 2 * (n_pts // 2) + b // 2

    side, seat = p % 2, place(p)
    here = pl.ds(side * (n_pts // 2), n_pts // 2)
    there = pl.ds((1 - side) * (n_pts // 2), n_pts // 2)

    def remote(source, target, send, recv, **to):
        return pltpu.make_async_remote_copy(
            src_ref=source, dst_ref=target, send_sem=send, recv_sem=recv,
            device_id=to, device_id_type=MESH,
        )

    def start(copies):
        for copy in copies:
            copy.start()

    def wait(copies):
        for copy in copies:
            copy.wait()

    def x_block(owner, row0, size):
        return xf.at[place(owner), pl.ds(row0, size)]

    def v_block(owner, row0, size):
        return vf.at[:, pl.ds(pl.multiple_of(owner * vr + row0, size), size)]

    def gather_link(block_of, row0, size, step, ident, send, recv):
        out = []
        for a, order in enumerate(orders):
            for i, d in enumerate(spans(order[:step])):
                at = (1 << step) - 1 + i
                block = block_of(p ^ d, row0 + a * (size // m), size // m)
                out.append(remote(block, block, send.at[ident, a, at], recv.at[ident, a, at],
                                  pts=p ^ (1 << order[step])))
        return out

    def gather_near(block_of, row0, size, ident, send, recv):
        out = []
        for i, d in enumerate(near_owners):
            block = block_of(p ^ d, row0, size)
            out.append(remote(block, block, send.at[ident, i], recv.at[ident, i], pts=p ^ 1))
        return out

    def spread_near(row0, size, ident):
        part = xf.at[here, pl.ds(row0, size)]
        return [remote(part, part, acs.at[ident, 0], acr.at[ident, 0], pts=p ^ 1)]

    def reduce_near(c):
        rows = pl.ds(c * ck, ck)
        return [remote(df.at[there, rows], near.at[:, rows], rcs.at[c, 0], rcr.at[c, 0], pts=p ^ 1)]

    def reduce_link(c, step):
        out = []
        for a, order in enumerate(orders):
            rows = pl.ds(c * ck + a * (ck // m), ck // m)
            to = p ^ (1 << order[step])
            for i, d in enumerate(spans(order[:step])):
                at = (1 << step) - 1 + i
                out.append(remote(df.at[place(to ^ d), rows], far.at[at, rows], rls.at[c, a, at],
                                  rlr.at[c, a, at], pts=to))
        return out

    def add_near(c):
        rows = pl.ds(c * ck, ck)
        df[here, rows] = df[here, rows] + near[:, rows]

    def add_link(c, step):
        for a, order in enumerate(orders):
            rows = pl.ds(c * ck + a * (ck // m), ck // m)
            for i, d in enumerate(spans(order[:step])):
                at = (1 << step) - 1 + i
                slot = place(p ^ d)
                df[slot, rows] = df[slot, rows] + far[at, rows]

    def line_block(sign, r, sending):
        if sign > 0:
            block = j - r if sending else j - 1 - r
            edge = (j < last) if sending else (j > 0)
            ok = edge & (block >= 0)
        else:
            block = j + r if sending else j + 1 + r
            edge = (j > 0) if sending else (j < last)
            ok = edge & (block <= last)
        return jnp.clip(block, 0, last), ok

    def line_copy(item, sign, r, sending, first=None):
        block, ok = line_block(sign, r, sending)
        target, send, recv = item(block, 0 if sign > 0 else 1, r)
        source = first if (first is not None and r == 0 and sending) else target
        to = jnp.clip(j + sign, 0, last)
        return remote(source, target, send, recv, val=to), ok

    def x_item(block, way, r):
        return xf.at[seat, pl.ds(block * vb, vb)], zsx.at[0, way, r], zrx.at[0, way, r]

    def e_item(block, way, r):
        return ef.at[block], zsx.at[1, way, r], zrx.at[1, way, r]

    def c_item(k):
        def item(block, way, r):
            return cf.at[block, k], zs.at[way, r, k], zr.at[way, r, k]

        return item

    def wanted(k, sign, sending):
        to = j + sign if sending else j
        return (k != SERVED) | ((to > 0) & (to < last))

    def line_do(what, item, sign, r, first=None, k=None):
        copy, ok = line_copy(item, sign, r, what != "recv", first)
        if k is not None and serving:
            ok = ok & wanted(k, sign, what != "recv")

        @pl.when(ok)
        def _():
            if what == "start":
                copy.start()
            elif what == "recv":
                copy.wait_recv()
            else:
                copy.wait_send()

    def columns(k):
        return pl.ds(pl.multiple_of(k * qc, qc), qc)

    own = [
        pltpu.make_async_copy(v_ref.at[:, pl.ds(t * cw, cw)], vf.at[t, pl.ds(p * vr, vr)],
                              local.at[4 + nk + t])
        for t in range(n_pts)
    ]
    first = [
        pltpu.make_async_copy(x_ref, xf.at[seat, pl.ds(j * vb, vb)], local.at[0]),
        pltpu.make_async_copy(x_ref, xo, local.at[1]),
        pltpu.make_async_copy(w_ref, wf, local.at[2]),
    ]
    mine = [
        pltpu.make_async_copy(c_ref.at[:, pl.ds(k * qc, qc)], cf.at[j, k], local.at[4 + k])
        for k in range(nk)
    ]
    start(own)
    start(first[:2])
    start(mine)
    start(first[2:])
    ef[j] = jnp.broadcast_to(e_ref[...], ef.shape[1:])

    barrier = pltpu.get_barrier_semaphore()
    for bit in [0] + bits:
        pl.semaphore_signal(barrier, inc=1, device_id={"pts": p ^ (1 << bit)}, device_id_type=MESH)

    @pl.when(j > 0)
    def _():
        pl.semaphore_signal(barrier, inc=1, device_id={"val": j - 1}, device_id_type=MESH)

    @pl.when(j < last)
    def _():
        pl.semaphore_signal(barrier, inc=1, device_id={"val": j + 1}, device_id_type=MESH)

    @pl.when(depth == 0)
    def _():
        pl.semaphore_wait(barrier, m + 2)

    @pl.when(depth > 0)
    def _():
        pl.semaphore_wait(barrier, m + 3)

    def send_c(k):
        for sign in (1, -1):
            line_do("start", c_item(k), sign, 0, c_ref.at[:, pl.ds(k * qc, qc)], k)

    def x_round(r):
        for sign in (1, -1):
            for item in (x_item, e_item):
                line_do("recv", item, sign, r)
                if r + 1 < n_val - 1:
                    line_do("start", item, sign, r + 1)

    def split_c(block, k):
        for i in range(cr // cw):
            rows = pl.ds(pl.multiple_of(place(block * (cr // cw) + i) * cw, cw), cw)
            high, low = split(cf[block, k, i * cw:(i + 1) * cw])
            ch[rows, columns(k)] = high
            cl[rows, columns(k)] = low

    def arrive(r, k):
        for sign in (1, -1):
            line_do("recv", c_item(k), sign, r, None, k)
            if r + 1 < n_val - 1:
                line_do("start", c_item(k), sign, r + 1, None, k)
        for sign in (1, -1):
            block, ok = line_block(sign, r, False)
            if serving:
                ok = ok & wanted(k, sign, False)

            @pl.when(ok)
            def _():
                split_c(block, k)

    def split_own(k, carry):
        split_c(j, k)
        return carry

    def split_v(o, carry):
        rows = pl.ds(pl.multiple_of(o * vr, vr), vr)
        for t in range(n_pts):
            high, low = split(vf[t, rows])
            vh[rows, t * cw:(t + 1) * cw] = high
            vl[rows, t * cw:(t + 1) * cw] = low
        return carry

    def split_x(row0, size):
        rows = pl.ds(row0, size)
        for b in range(n_pts):
            high, low = split(xf[b, rows])
            xh[rows, b * cw:(b + 1) * cw] = high
            xl[rows, b * cw:(b + 1) * cw] = low

    def split_rows(t, carry):
        split_x(pl.multiple_of(t * ck, ck), ck)
        return carry

    def clear(t, carry):
        rows = pl.ds(pl.multiple_of(t * cr, cr), cr)
        for ref in (ch, cl):
            ref[rows, columns(SERVED)] = jnp.zeros((cr, qc), jnp.bfloat16)
        return carry

    for sign in (1, -1):
        line_do("start", x_item, sign, 0, x_ref)
        line_do("start", e_item, sign, 0)
    unsent = list(range(nk))
    heads = list(range(nk)) if n_val > 2 else []
    send_c(unsent.pop(0))
    wait(own)
    start(gather_link(v_block, 0, vr, 0, 0, vls, vlr))
    for r in range(n_val - 1):
        x_round(r)
        for k in unsent[: 1 if r < n_val - 3 else nk]:
            send_c(k)
        unsent = unsent[1:] if r < n_val - 3 else []
        if r == 0:
            for step in range(1, m):
                wait(gather_link(v_block, 0, vr, step - 1, 0, vls, vlr))
                start(gather_link(v_block, 0, vr, step, 0, vls, vlr))
            wait(mine)
            if serving:
                @pl.when(depth == 0)
                def _():
                    lax.fori_loop(0, nc // cr, clear, 0)

            lax.fori_loop(0, nk, split_own, 0)
        if 0 < r < n_val - 2 or n_val == 2:
            wait(gather_link(v_block, 0, vr, m - 1, 0, vls, vlr))
            start(gather_near(v_block, 0, vr, 0, vcs, vcr))
            if heads:
                arrive(0, heads.pop(0))
            wait(gather_near(v_block, 0, vr, 0, vcs, vcr))
            lax.fori_loop(0, n_pts, split_v, 0)
            if heads:
                arrive(0, heads.pop(0))
    first[0].wait()
    start(gather_link(x_block, 0, nv, 0, 0, als, alr))
    for step in range(1, m):
        wait(gather_link(x_block, 0, nv, step - 1, 0, als, alr))
        start(gather_link(x_block, 0, nv, step, 0, als, alr))
        if heads:
            arrive(0, heads.pop(0))
    wait(gather_link(x_block, 0, nv, m - 1, 0, als, alr))
    start(spread_near(0, nv, 0))
    for k in heads:
        arrive(0, k)
    wait(spread_near(0, nv, 0))
    lax.fori_loop(0, chunks, split_rows, 0)
    for r in range(n_val - 1):
        for sign in (1, -1):
            for item in (x_item, e_item):
                line_do("send", item, sign, r, x_ref if item is x_item else None)
    wait(first[1:])

    nt = min(512, nn)

    def store(high, low, at, value):
        a, b = split(value)
        high[at] = a
        low[at] = b

    def group_rows(g):
        return pl.ds(pl.multiple_of(g * gr, gr), gr)

    def pass_p(g):
        part = pbuf.at[group_rows(g)]
        return remote(part, part, ps.at[g], pr.at[g], val=outer)

    def pass_b(g):
        part = bbuf.at[group_rows(g)]
        return remote(part, part, bs.at[g], br.at[g], val=inner)

    def late(i):
        block = jnp.where(j < half, i + 1, i)
        part = cf.at[block, SERVED]
        return block, remote(part, part, ds.at[i], dr.at[i], val=outer)

    def first_product(g, cols):
        rows = group_rows(g)
        return product(((1,), (0,)), (xh[rows], xl[rows]), (ch[:, cols], cl[:, cols]))

    def serve(g, c):
        cols = columns(SERVED)
        value = first_product(g, cols)
        pbuf[group_rows(g)] = value
        pass_p(g).start()
        store(ph, pl_, (group_rows(g), cols), value)
        return c

    ahead = serving and cr == 2 * cw and n_pts == 2 * n_val

    def partial(g, cols, at, size):
        rows = group_rows(g)
        total = None
        for base in (0, n_val):
            some = pl.ds(pl.multiple_of((at + base) * cw, cw), size * cw)
            value = product(
                ((1,), (0,)), (xh[rows, some], xl[rows, some]), (ch[some, cols], cl[some, cols]))
            total = value if total is None else total + value
        return total

    def column(k, ending=False):
        cols = columns(k)
        served = (k == SERVED) if serving else (k < 0)
        alone = jnp.logical_not(served & (depth <= 1))

        def pair(g, c):
            store(ph, pl_, (group_rows(g), cols), first_product(g, cols))
            return c

        begun = (k > SERVED) & (depth == 0) if ahead and ending else (k < 0)

        @pl.when(alone & jnp.logical_not(begun))
        def _():
            lax.fori_loop(0, groups, pair, 0)

        if ahead and ending:
            def complete(g, c):
                value = partial(g, cols, jnp.where(j == 0, last, 0), 1)
                store(ph, pl_, (group_rows(g), cols), pbuf[group_rows(g)] + value)
                return c

            @pl.when(begun)
            def _():
                lax.fori_loop(0, groups, complete, 0)

        def taken(g, c):
            pass_p(g).wait_recv()
            store(ph, pl_, (group_rows(g), cols), pbuf[group_rows(g)])
            return c

        if serving:
            @pl.when(served & (depth == 0))
            def _():
                lax.fori_loop(0, groups, taken, 0)

        def mixed(t, c):
            at = pl.ds(pl.multiple_of(t * nt, nt), nt)
            value = product(((0,), (0,)), (vh[:, at], vl[:, at]), (ph[:, cols], pl_[:, cols]))
            store(zh, zl, (at, cols), value * wf[at, cols])
            return c

        lax.fori_loop(0, nn // nt, mixed, 0)

        def back(g, c):
            rows = group_rows(g)
            value = product(((1,), (0,)), (vh[rows], vl[rows]), (zh[:, cols], zl[:, cols]))

            if serving:
                @pl.when(served & (depth == 0))
                def _():
                    bbuf[rows] = value
                    pass_b(g).start()
                    ph[rows, cols] = jnp.zeros((gr, qc), jnp.bfloat16)
                    pl_[rows, cols] = jnp.zeros((gr, qc), jnp.bfloat16)

                @pl.when(served & (depth == 1))
                def _():
                    pass_b(g).wait_recv()
                    store(ph, pl_, (rows, cols), value + bbuf[rows])

            @pl.when(alone)
            def _():
                store(ph, pl_, (rows, cols), value)

            return c

        lax.fori_loop(0, groups, back, 0)

    for r in range(1, n_val - 2):
        def pass_on(k, carry):
            arrive(r, k)
            if r == n_val - 3:
                @pl.when((k == SERVED) & (depth == 1))
                def _():
                    lax.fori_loop(0, groups, serve, 0)

                @pl.when((k != SERVED) & (depth > 0))
                def _():
                    column(k)

            return carry

        lax.fori_loop(0, nk, pass_on, 0)

    def late_start(some):
        if serving:
            @pl.when(depth == 1)
            def _():
                for i in some:
                    late(i)[1].start()

    late_start(range(last)[:LATE_NOW])

    def finish_column(k, carry):
        if ahead:
            def early(g, c):
                pbuf[group_rows(g)] = partial(
                    g, columns(k), jnp.where(j == 0, 0, 1), n_val - 1)
                return c

            @pl.when((k > SERVED) & (depth == 0))
            def _():
                lax.fori_loop(0, groups, early, 0)

        arrive(n_val - 2, k)
        if serving:
            @pl.when((k == SERVED) | (depth == 0))
            def _():
                column(k, True)
        else:
            column(k)
        return carry

    lax.fori_loop(0, nk, finish_column, 0)

    def sent(k, carry):
        for r in range(n_val - 1):
            for sign in (1, -1):
                line_do("send", c_item(k), sign, r, c_ref.at[:, pl.ds(0, qc)], k)
        return carry

    lax.fori_loop(0, nk, sent, 0)
    if serving:
        for g in range(groups):
            @pl.when(depth == 1)
            def _():
                pass_p(g).wait_send()

            @pl.when(depth == 0)
            def _():
                pass_b(g).wait_send()

    def late_end():
        if not serving:
            return
        for i in range(last):
            @pl.when(depth == 1)
            def _():
                late(i)[1].wait_send()

            @pl.when(depth == 0)
            def _():
                block, copy = late(i)
                copy.wait_recv()
                split_c(block, SERVED)

    def direct(g, flip):
        rows = pl.ds(g * gr, gr)

        half_at = (p + flip) % 2 * (n_pts // 2)

        def body(t, c):
            at = pl.ds(pl.multiple_of((half_at + 2 * t) * cw, 2 * cw), 2 * cw)
            value = product(((1,), (1,)), (ph[rows], pl_[rows]), (ch[at], cl[at]))
            df[half_at + 2 * t, rows] = value[:, :cw]
            df[half_at + 2 * t + 1, rows] = value[:, cw:]
            return c

        lax.fori_loop(0, n_pts // 4, body, 0)

    def reduce_stages(c):
        stages = [lambda: (wait(reduce_near(c)), add_near(c), start(reduce_link(c, m - 1)))]
        for step in range(m - 1, 0, -1):
            stages.append(lambda step=step: (
                wait(reduce_link(c, step)), add_link(c, step), start(reduce_link(c, step - 1))))
        return stages

    def last_add(c):
        wait(reduce_link(c, 0))
        add_link(c, 0)

    def own_sum(c):
        rows = pl.ds(c * ck, ck)
        return df[seat, rows]

    def scaled(c, newer, total):
        row0 = c % SUB * ck
        ediff = cond_ref[...] - ef[c // SUB].T[row0:row0 + ck, 0:1]
        hamil = ediff * newer - total
        return (hamil - CENTER * newer) / HALF_WIDTH

    def spread_stages(c):
        rows = pl.ds(c * ck, ck)
        stages = reduce_stages(c)
        source = df.at[seat, rows]

        def to_inner():
            return remote(source, zin.at[rows], hs.at[c, 0], hr.at[c, 0], val=inner)

        def across():
            return remote(source, zx.at[rows], hs.at[c, 0], hr.at[c, 1], val=inner)

        def to_outer():
            return remote(zx.at[rows], zx.at[rows], hs.at[c, 1], hr.at[c, 1], val=outer)

        def inward(i):
            if i == 0:
                last_add(c)

            @pl.when(depth == i)
            def _():
                if i > 0:
                    to_inner().wait_recv()
                    df[seat, rows] = df[seat, rows] + zin[rows]
                (across() if i == half - 1 else to_inner()).start()

        def outward(i):
            @pl.when(depth == i)
            def _():
                across().wait_recv()
                if i == half - 1:
                    zx[rows] = zx[rows] + df[seat, rows]
                if i > 0:
                    to_outer().start()

        def following():
            across().wait_send()

            @pl.when(depth > 0)
            def _():
                to_outer().wait_send()

            newer = xf[seat, rows]
            xf[seat, rows] = scaled(c, newer, zx[rows])
            start(gather_link(x_block, c * ck, ck, 0, c, als, alr))

        for i in range(half):
            stages.append(lambda i=i: inward(i))
        for i in range(half - 1, 0, -1):
            stages.append(lambda i=i: outward(i))
        stages.append(lambda: (outward(0), following()))
        for step in range(1, m):
            stages.append(lambda step=step: (
                wait(gather_link(x_block, c * ck, ck, step - 1, c, als, alr)),
                start(gather_link(x_block, c * ck, ck, step, c, als, alr))))
        stages.append(lambda: (
            wait(gather_link(x_block, c * ck, ck, m - 1, c, als, alr)),
            start(spread_near(c * ck, ck, c))))
        stages.append(lambda: (
            wait(spread_near(c * ck, ck, c)), split_x(c * ck, ck)))
        return stages

    def final_stages(c):
        rows = pl.ds(c * ck, ck)
        owner, part = c // SUB, pl.ds(c % SUB * ck, ck)
        stages = reduce_stages(c)

        def right():
            return remote(df.at[seat, rows], fin.at[rows], fs.at[c, 0], fr.at[c, 0],
                          val=jnp.minimum(j + 1, last))

        def left():
            return remote(df.at[seat, rows], fx.at[rows], fs.at[c, 0], fr.at[c, 1],
                          val=jnp.maximum(j - 1, 0))

        def step(i):
            if i == 0:
                last_add(c)
            if i < owner:
                @pl.when(j == i)
                def _():
                    if i > 0:
                        right().wait_recv()
                        df[seat, rows] = df[seat, rows] + fin[rows]
                    right().start()
            if last - i > owner:
                @pl.when(j == last - i)
                def _():
                    if i > 0:
                        left().wait_recv()
                        df[seat, rows] = df[seat, rows] + fx[rows]
                    left().start()

        def finish():
            @pl.when(j == owner)
            def _():
                total = df[seat, rows]
                if owner > 0:
                    right().wait_recv()
                    total = total + fin[rows]
                if owner < last:
                    left().wait_recv()
                    total = total + fx[rows]
                out_ref[part] = 2.0 * scaled(c, xf[seat, rows], total) - xo[part]

            @pl.when(j != owner)
            def _():
                right().wait_send()

        for i in range(max(owner, last - owner)):
            stages.append(lambda i=i: step(i))
        stages.append(finish)
        return stages

    per = chunks // groups

    def reduction(stages_of, order, fillers, begins, gap):
        direct(0, 1)
        for c in order[:per]:
            start(reduce_near(c))
        direct(0, 0)
        todo = {c: (begin, stages_of(c)) for begin, c in zip(begins, order)}
        end = max(b + gap * (len(s) - 1) + 1 for b, s in todo.values())
        for tick in range(end):
            if tick in fillers:
                fillers[tick]()
            for c in order:
                b, stages = todo[c]
                at, rest = divmod(tick - b, gap)
                if rest == 0 and 0 <= at < len(stages):
                    stages[at]()

    def near_rest(order):
        for c in order[per:]:
            start(reduce_near(c))

    qt = min(512, q)

    def pair(g, begin, end):
        rows = pl.ds(g * gr, gr)

        def body(t, c):
            at = pl.ds(pl.multiple_of(t * qt, qt), qt)
            store(ph, pl_, (rows, at), product(
                ((1,), (0,)), (xh[rows], xl[rows]), (ch[:, at], cl[:, at])))
            return c

        lax.fori_loop(begin, end, body, 0)

    order = list(range(chunks))
    begins = begin_ticks(chunks, SPREAD)
    stages = len(spread_stages(0))
    full = begins[per - 1] + GAP * (stages - 1) + 1
    freed = begins[-1] + GAP * (stages - 5) + 1
    fillers = {
        0: lambda: direct(1, 1), 1: lambda: near_rest(order), 2: lambda: direct(1, 0),
        freed: lambda: late_start(range(last)[LATE_NOW:]), full: lambda: pair(0, 1, q // qt)}
    reduction(spread_stages, order, fillers, begins, GAP)
    pair(1, 1, q // qt)
    late_end()
    pair(0, 0, 1)
    pair(1, 0, 1)

    def mixed(t, c):
        at = pl.ds(pl.multiple_of((t // (q // qt)) * nt, nt), nt)
        cols = pl.ds(pl.multiple_of((t % (q // qt)) * qt, qt), qt)
        value = product(((0,), (0,)), (vh[:, at], vl[:, at]), (ph[:, cols], pl_[:, cols]))
        store(zh, zl, (at, cols), value * wf[at, cols])
        return c

    lax.fori_loop(0, (nn // nt) * (q // qt), mixed, 0)

    def back(g):
        def body(t, c):
            rows = pl.ds(g * gr, gr)
            at = pl.ds(pl.multiple_of(t * qt, qt), qt)
            store(ph, pl_, (rows, at), product(
                ((1,), (0,)), (vh[rows], vl[rows]), (zh[:, at], zl[:, at])))
            return c

        lax.fori_loop(0, q // qt, body, 0)

    back(0)
    order = order[:per] + order[per:][::-1]
    reduction(final_stages, order, {
        0: lambda: back(1), 1: lambda: direct(1, 1), 2: lambda: (near_rest(order), direct(1, 0)),
    }, begin_ticks(chunks, FINAL), FINAL_GAP)


def fused(n_pts, n_val, vectors, eval_energy, cond_energy, val_orbitals, cond_orbitals, screened):
    vb, cw = vectors.shape[1:]
    vr, nn = val_orbitals.shape
    cr, q = cond_orbitals.shape
    nv, nc = vb * n_val, cw * n_pts
    nk = q // QC
    m = n_pts.bit_length() - 2
    f32, bf16 = jnp.float32, jnp.bfloat16
    links, chunks = (1 << m) - 1, n_val * SUB
    any_, dma = pl.BlockSpec(memory_space=pl.ANY), pltpu.SemaphoreType.DMA
    vmem = pl.BlockSpec(memory_space=pltpu.VMEM)
    buffers = [
        ((n_val, nk, cr, QC), f32), ((nc, q), bf16), ((nc, q), bf16), ((nn, q), f32),
        ((n_pts, nv, cw), f32), ((nv, nn), bf16), ((nv, nn), bf16),
        ((n_pts, nv, cw), f32), ((nv, nc), bf16), ((nv, nc), bf16),
        ((nv, q), bf16), ((nv, q), bf16), ((nn, q), bf16), ((nn, q), bf16),
        ((n_pts // 2, nv, cw), f32), ((links, nv, cw), f32),
        ((nv, cw), f32), ((nv, cw), f32), ((nv, cw), f32), ((nv, cw), f32), ((vb, cw), f32),
        ((n_val, 8, vb), f32), ((nv, QC), f32), ((nv, QC), f32),
    ]
    semaphores = [
        (4 + nk + n_pts,), (2, n_val - 1, nk), (2, n_val - 1, nk), (2, 2, n_val - 1), (2, 2, n_val - 1),
        (1, m, links), (1, m, links), (1, n_pts // 2), (1, n_pts // 2),
        (chunks, m, links), (chunks, m, links), (chunks, n_pts // 2), (chunks, n_pts // 2),
        (chunks, m, links), (chunks, m, links), (chunks, n_pts // 2), (chunks, n_pts // 2),
        (chunks, 2), (chunks, 2),
        (2,), (2,), (2,), (2,), (n_val - 1,), (n_val - 1,),
        (chunks, 2), (chunks, 2),
    ]
    out = pl.pallas_call(
        functools.partial(fused_kernel, n_pts, n_val),
        out_shape=jax.ShapeDtypeStruct((vb, cw), f32),
        in_specs=[any_, vmem, vmem, any_, any_, any_],
        out_specs=vmem,
        scratch_shapes=[pltpu.VMEM(*b) for b in buffers] + [dma(s) for s in semaphores],
        compiler_params=pltpu.CompilerParams(
            collective_id=0, has_side_effects=True, vmem_limit_bytes=VMEM_BYTES
        ),
    )(
        vectors[0], eval_energy[None], cond_energy[None],
        val_orbitals, cond_orbitals, screened,
    )
    return out[None]


def fits(n_pts, n_val, vectors, val_orbitals, cond_orbitals):
    vb, cw = vectors.shape[1:]
    vr, nn = val_orbitals.shape
    cr, q = cond_orbitals.shape
    nv, nc = vb * n_val, cw * n_pts
    m = n_pts.bit_length() - 2
    if n_pts & (n_pts - 1) or m < 1 or n_val % 2 or n_val < 2:
        return False
    if nn != nc or vb % LANES:
        return False
    if q // QC <= SERVED + 1:
        return False
    if cr % cw or (SERVED + 1) * QC > 512:
        return False
    if cw % LANES or q % QC or nn % 512 or vb % (16 * m * SUB) or vr % (16 * m) or cr % 16:
        return False
    held = 8 * nc * q + 8 * nn * q + 8 * nv * nn + 4 * nv * nc + 4 * nv * q
    held += 4 * nv * nc * 3 // 2 + 4 * nv * cw * ((1 << m) + 3)
    held += 8 * nv * QC
    return held <= VMEM_BYTES - 3 * 2**20


def solution(mesh):
    placed = (
        P(None, "val", "pts"),
        P("val"),
        P("pts"),
        P("pts", "val"),
        P("val", "pts"),
        P("val", "pts"),
    )
    n_pts, n_val = mesh.shape["pts"], mesh.shape["val"]

    def body(vectors, eval_energy, cond_energy, val_orbitals, cond_orbitals, screened):
        run = fused if fits(n_pts, n_val, vectors, val_orbitals, cond_orbitals) else per_device
        return run(
            n_pts, n_val, vectors, eval_energy, cond_energy, val_orbitals, cond_orbitals, screened
        )

    return jax.shard_map(
        body, mesh=mesh, in_specs=placed, out_specs=P(None, "val", "pts"), check_vma=False
    )
```
